512 devices in a mesh: mirror: 2 (over y_hi), rows: 64 (over z, y_lo, core), cols: 4 (over x).
Axes of the slice: x: 4, y: 8 (y_hi: 2, y_lo: 4; y = y_hi * 4 + y_lo), z: 8, core: 2. Of those that a mesh axis runs over, the one named last changes fastest.
Arguments:
- currents: bfloat16 [16, 131072], P(None, ('mirror', 'rows')), may hold values from -6 to 6
- right_side: float32 [16, 131072], P(None, ('mirror', 'rows', 'cols')), may hold values from -6 to 6
- geometry: float32 [4, 65536], replicated, may hold values from 0 to 4, as said below
Outputs:
- residual: float32 [16, 131072], P(None, ('mirror', 'rows', 'cols'))
- krylov_image: float32 [16, 131072], P(None, ('mirror', 'rows', 'cols'))
The draws below stay inside these ranges and needn't reach their ends.
Inputs may be any that keep to these rules, and one draw needn't show every extreme that they name: `geometry`: rows are x in [0, 1], y in [0.05, 0.45], z in [0, 4] and a size in [0.003, 0.03].
All inputs are finite; a program needn't handle non-finite values.
Results may differ from the reference program's by a relative error of at most 0.0024.
Values may be sent and summed in bfloat16 or wider, within the bound.
A program may use at most 64 MiB of HBM per device.

```python
import math
import jax
import jax.numpy as jnp
from jax import lax

CELLS = 131072
HALF = 65536
RHS = 16


def draw_geometry(key, part):
    keys = jax.random.split(key, 4)
    across = jax.random.uniform(keys[0], (HALF,), jnp.float32, 0.0, 1.0)
    height = jax.random.uniform(keys[1], (HALF,), jnp.float32, 0.05, 0.45)
    depth = jax.random.uniform(keys[2], (HALF,), jnp.float32, 0.0, 4.0)
    log_size = jax.random.uniform(keys[3], (HALF,), jnp.float32, jnp.log(0.003), jnp.log(0.03))
    sizes = jnp.clip(jnp.exp(log_size), 0.003, 0.03)
    return jnp.stack([across, height, depth, sizes])


def levels(key, extent, shards, smallest, largest):
    def one(axis_at, shards_of):
        steps = jax.random.uniform(jax.random.fold_in(jax.random.fold_in(key, 6), axis_at), (shards_of,), jnp.float32, smallest / len(shards), largest / len(shards))
        return jnp.repeat(jnp.exp(steps), extent[axis_at] // shards_of).reshape((-1,) + (1,) * (len(extent) - axis_at - 1))

    gain = one(*shards[0])
    for cut in shards[1:]:
        gain = gain * one(*cut)
    return gain


def normal_values(stream_key, extent, deviation, limit, shards=(), held_as=jnp.bfloat16):
    values = jax.random.normal(stream_key, extent, jnp.float32) * deviation
    if len(shards) > 0:
        values = levels(stream_key, extent, shards, -0.22, 0.18) * values
    return jnp.clip(values, min=-limit, max=limit).astype(held_as)


def setup_inputs(seed: int = 0) -> dict:
    key_list = jax.random.split(jax.random.key(seed), 4)
    currents = normal_values(key_list[0], (RHS, CELLS), 1.0, 6.0, ((1, 128),))
    right_side = normal_values(key_list[1], (RHS, CELLS), 1.0, 6.0, ((1, 512),), jnp.float32)
    geometry = draw_geometry(jax.random.fold_in(key_list[3], 71), 0)
    return dict(currents=currents, right_side=right_side, geometry=geometry)


def kernel_block(row_geo, col_geo, reflect, scaling):
    diff_x = row_geo[0][:, None] - col_geo[0][None, :]
    diff_y = row_geo[1][:, None] - reflect * col_geo[1][None, :]
    diff_z = row_geo[2][:, None] - col_geo[2][None, :]
    spread = (row_geo[3] * row_geo[3])[:, None] + (col_geo[3] * col_geo[3])[None, :]
    squared = diff_x * diff_x + diff_y * diff_y + diff_z * diff_z + spread
    return (scaling / jnp.sqrt(squared)).astype(jnp.bfloat16)

def apply_operator(currents_in, geometry):
    scaling = 1.0 / math.sqrt(CELLS)
    first_cur = currents_in[:, :HALF].astype(jnp.float32)
    second_cur = currents_in[:, HALF:].astype(jnp.float32)
    block_len = min(512, HALF)
    block_count = HALF // block_len

    def one_block(position):
        offset = position * block_len
        geo_part = lax.dynamic_slice_in_dim(geometry, offset, block_len, 1)
        self_tile = kernel_block(geo_part, geometry, 1.0, scaling)
        mirror_tile = kernel_block(geo_part, geometry, -1.0, scaling)
        self_tile = lax.optimization_barrier(self_tile).astype(jnp.float32)
        mirror_tile = lax.optimization_barrier(mirror_tile).astype(jnp.float32)
        upper = jnp.dot(first_cur, self_tile.T, precision=lax.Precision.HIGHEST, preferred_element_type=jnp.float32) + jnp.dot(second_cur, mirror_tile.T, precision=lax.Precision.HIGHEST, preferred_element_type=jnp.float32)
        lower = jnp.dot(second_cur, self_tile.T, precision=lax.Precision.HIGHEST, preferred_element_type=jnp.float32) + jnp.dot(first_cur, mirror_tile.T, precision=lax.Precision.HIGHEST, preferred_element_type=jnp.float32)
        return (upper, lower)
    upper_all, lower_all = lax.map(one_block, jnp.arange(block_count, dtype=jnp.int32))
    excite = currents_in.shape[0]
    upper_all = jnp.transpose(upper_all, (1, 0, 2)).reshape(excite, HALF)
    lower_all = jnp.transpose(lower_all, (1, 0, 2)).reshape(excite, HALF)
    return jnp.concatenate([upper_all, lower_all], axis=1)

def reference(currents, right_side, geometry):
    voltage = apply_operator(currents, geometry)
    residual = right_side - voltage
    residual_b = residual.astype(jnp.bfloat16)
    krylov_image = apply_operator(residual_b, geometry)
    return (residual, krylov_image)
```

```python
import functools

import jax
import jax.numpy as jnp
from jax import lax
from jax.experimental import pallas as pl
from jax.experimental.pallas import tpu as pltpu
from jax.sharding import PartitionSpec as P

MESH = pl.DeviceIdType.MESH
F32, BF16 = jnp.float32, jnp.bfloat16
HALF = 65536
RHS = 16
PIECE = 256
SOURCES = 4096
TARGETS = 2048
PIECES = SOURCES // PIECE
BLOCKS = TARGETS // PIECE
TERMS = 32
SQUARE = 2.0**17
ROOT = 2.0**8.5
CHUNK = 256
SENDERS = 16


def split3(value):
    high = value.astype(BF16).astype(F32)
    rest = value - high
    middle = rest.astype(BF16).astype(F32)
    return high, middle, (rest - middle).astype(BF16).astype(F32)


def store_terms(geo, terms, source):
    across = geo[0:1, :] - 0.5
    height = geo[1:2, :] - 0.25
    size = geo[3:4, :]
    own = across * across + height * height + size * size
    xs, ys, qs = split3(across), split3(height), split3(own)
    one = jnp.ones_like(across)
    if source:
        zs = split3(geo[2:3, :] - 2.0)
        rows = [v[i] for v in (xs, ys) for i in (0, 0, 1, 0, 2, 1)]
        rows += [*qs, one, one, one, *zs]
    else:
        rows = [v[i] * (-2.0 * SQUARE) for v in (xs, ys) for i in (0, 1, 0, 2, 0, 1)]
        rows += [one * SQUARE] * 3 + [v * SQUARE for v in qs]
    for k in range(TERMS):
        terms[k : k + 1, :] = rows[k] if k < len(rows) else jnp.zeros_like(across)


def kernel(
    cur_ref, right_ref, geo_ref, res_ref, img_ref,
    a_ref, b_ref, gs_ref, gt_ref, fs_ref, ft_ref, l_ref, r_ref, zb_ref, yb_ref, zt_ref,
    own_ref, j_ref, v_ref, p_ref,
    geo_sem, gather_send, gather_recv, part_send, part_recv,
):
    mirror = lax.axis_index("mirror")
    row = lax.axis_index("rows")
    col = lax.axis_index("cols")
    core = row % 2
    home = row // 32
    slot = (row % 32) // 2
    area = row // 2
    me = mirror * 8 + core * 4 + col
    mine = core * 4 + col

    barrier = pltpu.get_barrier_semaphore()

    def greet_source(k, carry):
        for half in range(2):
            other = mirror * 32 + 2 * k + core

            @pl.when(jnp.logical_or(other != row, mirror != half))
            def _():
                pl.semaphore_signal(barrier, inc=1, device_id=(half, other, col), device_id_type=MESH)

        return carry

    lax.fori_loop(0, PIECES, greet_source, 0)

    def greet_part(k, carry):
        @pl.when(k != me)
        def _():
            pl.semaphore_signal(
                barrier, inc=1, device_id=(k // 8, area * 2 + (k // 4) % 2, k % 4), device_id_type=MESH
            )

        return carry

    lax.fori_loop(0, SENDERS, greet_part, 0)

    def source_geo(k, carry):
        start = pl.multiple_of((mirror * 32 + 2 * k + core) * 1024 + col * PIECE, PIECE)
        into = pl.multiple_of(k * PIECE, PIECE)
        pltpu.make_async_copy(
            geo_ref.at[:, pl.ds(start, PIECE)], gs_ref.at[:, pl.ds(into, PIECE)], geo_sem.at[0]
        ).start()
        return carry

    lax.fori_loop(0, PIECES, source_geo, 0)
    first = pl.multiple_of(area * TARGETS, TARGETS)
    target_geo = pltpu.make_async_copy(geo_ref.at[:, pl.ds(first, TARGETS)], gt_ref, geo_sem.at[1])
    target_geo.start()
    own_ref[0] = cur_ref[:, pl.ds(pl.multiple_of(col * PIECE, PIECE), PIECE)]
    pltpu.make_async_copy(geo_ref.at[:, pl.ds(0, SOURCES)], gs_ref, geo_sem.at[0]).wait()
    target_geo.wait()

    def gather_copy(which, j):
        into = pl.multiple_of(slot * PIECE, PIECE)
        return pltpu.make_async_remote_copy(
            src_ref=own_ref.at[which],
            dst_ref=j_ref.at[which, pl.ds(pl.multiple_of(mirror * RHS, RHS), RHS), pl.ds(into, PIECE)],
            send_sem=gather_send.at[which, j],
            recv_sem=gather_recv.at[which],
            device_id=(home, 2 * j + core, col),
            device_id_type=MESH,
        )

    def is_self(j):
        return jnp.logical_and(home == mirror, 2 * j + core == row)

    def gather_start(which):
        def send(i, carry):
            j = (area + i) % 32

            @pl.when(jnp.logical_not(is_self(j)))
            def _():
                gather_copy(which, j).start()

            @pl.when(is_self(j))
            def _():
                into = pl.multiple_of(slot * PIECE, PIECE)
                pltpu.make_async_copy(
                    own_ref.at[which],
                    j_ref.at[which, pl.ds(pl.multiple_of(mirror * RHS, RHS), RHS), pl.ds(into, PIECE)],
                    gather_recv.at[which],
                ).start()

            return carry

        lax.fori_loop(0, 32, send, 0)

    def gather_wait(which):
        pltpu.make_async_copy(j_ref.at[which], j_ref.at[which], gather_recv.at[which]).wait()

    def part_copy(which, half, block):
        start = pl.multiple_of(block * PIECE, PIECE)
        return pltpu.make_async_remote_copy(
            src_ref=v_ref.at[which, pl.ds(half * RHS, RHS), pl.ds(start, PIECE)],
            dst_ref=p_ref.at[which, me],
            send_sem=part_send.at[which, half, block],
            recv_sem=part_recv.at[which],
            device_id=(half, area * 2 + block // 4, block % 4),
            device_id_type=MESH,
        )

    def part_store(which, block, total):
        start = pl.multiple_of(block * PIECE, PIECE)
        v_ref[which, :, pl.ds(start, PIECE)] = total
        for half in range(2):

            @pl.when(jnp.logical_or(block != mine, mirror != half))
            def _():
                part_copy(which, half, block).start()

        @pl.when(jnp.logical_and(block == mine, mirror == 0))
        def _():
            p_ref[which, me] = total[0:RHS]

        @pl.when(jnp.logical_and(block == mine, mirror == 1))
        def _():
            p_ref[which, me] = total[RHS : 2 * RHS]

    def part_sum(which):
        others = p_ref.at[which, 0 : SENDERS - 1]
        pltpu.make_async_copy(others, others, part_recv.at[which]).wait()
        total = p_ref[which, 0]
        for k in range(1, SENDERS):
            total += p_ref[which, k]
        return total

    store_terms(gs_ref, fs_ref, True)
    store_terms(gt_ref, ft_ref, False)
    r_ref[...] = ft_ref[...].astype(BF16)
    zt_ref[0:1, :] = (gt_ref[2:3, :] - 2.0) * ROOT
    zt_ref[1:2, :] = gt_ref[1:2, :]
    l_ref[...] = jnp.transpose(fs_ref[...]).astype(BF16)
    term = lax.broadcasted_iota(jnp.int32, (TERMS, 128), 0)
    pick_z = ((term >= 18) & (term < 21)).astype(BF16)
    pick_y = ((term == 6) | (term == 10) | (term == 11)).astype(BF16)

    def spread(i, carry):
        at = pl.ds(pl.multiple_of(i * 512, 512), 512)
        left = l_ref[at, :]
        zb_ref[at, :] = jnp.dot(left, pick_z, preferred_element_type=F32) * ROOT
        yb_ref[at, :] = (jnp.dot(left, pick_y, preferred_element_type=F32) + 0.25) * (4.0 * SQUARE)
        return carry

    lax.fori_loop(0, SOURCES // 512, spread, 0)

    def make_tile(at, block):
        start = pl.multiple_of(block * PIECE, PIECE)
        rest = jnp.dot(l_ref[at, :], r_ref[:, pl.ds(start, PIECE)], preferred_element_type=F32)
        zb, yb = zb_ref[at, :], yb_ref[at, :]
        near, far = [], []
        for c in range(PIECE // 128):
            lanes = pl.ds(start + c * 128, 128)
            dz = zb - zt_ref[0:1, lanes]
            squared = dz * dz + rest[:, c * 128 : (c + 1) * 128]
            near.append(lax.rsqrt(squared).astype(BF16))
            far.append(lax.rsqrt(squared + yb * zt_ref[1:2, lanes]).astype(BF16))
        near, far = jnp.concatenate(near, 1), jnp.concatenate(far, 1)
        a_ref[at, pl.ds(start, PIECE)] = near
        b_ref[at, pl.ds(start, PIECE)] = far
        return near, far

    def swap(value):
        return jnp.concatenate([value[RHS:], value[:RHS]], 0)

    def build(block):
        def step(i, carry):
            make_tile(pl.ds(pl.multiple_of(i * CHUNK, CHUNK), CHUNK), block)
            return carry

        lax.fori_loop(0, SOURCES // CHUNK, step, 0, unroll=8)

    def build_and_apply(block):
        def step(i, total):
            at = pl.ds(pl.multiple_of(i * CHUNK, CHUNK), CHUNK)
            near, far = make_tile(at, block)
            part = j_ref[0, :, at]
            total += jnp.dot(part, near, preferred_element_type=F32)
            return total + swap(jnp.dot(part, far, preferred_element_type=F32))

        zero = jnp.zeros((2 * RHS, PIECE), F32)
        return lax.fori_loop(0, SOURCES // CHUNK, step, zero, unroll=SOURCES // CHUNK)

    def apply(which, block):
        at = pl.ds(pl.multiple_of(block * PIECE, PIECE), PIECE)
        part = j_ref[which]
        return jnp.dot(part, a_ref[:, at], preferred_element_type=F32) + swap(
            jnp.dot(part, b_ref[:, at], preferred_element_type=F32)
        )

    pl.semaphore_wait(barrier, jnp.where(home == mirror, 31, 32) + SENDERS - 1)
    gather_start(0)
    build(mine)
    gather_wait(0)

    def first(i, carry):
        block = (mine + 1 + i) % BLOCKS
        part_store(0, block, build_and_apply(block))
        return carry

    lax.fori_loop(0, BLOCKS - 1, first, 0)
    part_store(0, mine, apply(0, mine))
    residual = right_ref[...] - part_sum(0)
    res_ref[...] = residual
    own_ref[1] = residual.astype(BF16)

    gather_start(1)
    gather_wait(1)

    def second(i, carry):
        block = (mine + 1 + i) % BLOCKS
        part_store(1, block, apply(1, block))
        return carry

    lax.fori_loop(0, BLOCKS, second, 0)
    img_ref[...] = part_sum(1)

    for which in range(2):

        def gathered(j, carry):
            @pl.when(jnp.logical_not(is_self(j)))
            def _():
                gather_copy(which, j).wait_send()

            return carry

        lax.fori_loop(0, 32, gathered, 0)

        def parted(block, carry):
            for half in range(2):

                @pl.when(jnp.logical_or(block != mine, mirror != half))
                def _():
                    part_copy(which, half, block).wait_send()

            return carry

        lax.fori_loop(0, BLOCKS, parted, 0)


def on_device(currents, right_side, geometry):
    vmem = pl.BlockSpec(memory_space=pltpu.VMEM)
    owned = jax.ShapeDtypeStruct((RHS, PIECE), F32)
    return pl.pallas_call(
        kernel,
        out_shape=(owned, owned),
        in_specs=[vmem, vmem, pl.BlockSpec(memory_space=pl.ANY)],
        out_specs=(vmem, vmem),
        scratch_shapes=[
            pltpu.VMEM((SOURCES, TARGETS), BF16),
            pltpu.VMEM((SOURCES, TARGETS), BF16),
            pltpu.VMEM((4, SOURCES), F32),
            pltpu.VMEM((4, TARGETS), F32),
            pltpu.VMEM((TERMS, SOURCES), F32),
            pltpu.VMEM((TERMS, TARGETS), F32),
            pltpu.VMEM((SOURCES, TERMS), BF16),
            pltpu.VMEM((TERMS, TARGETS), BF16),
            pltpu.VMEM((SOURCES, 128), F32),
            pltpu.VMEM((SOURCES, 128), F32),
            pltpu.VMEM((2, TARGETS), F32),
            pltpu.VMEM((2, RHS, PIECE), BF16),
            pltpu.VMEM((2, 2 * RHS, SOURCES), BF16),
            pltpu.VMEM((2, 2 * RHS, TARGETS), F32),
            pltpu.VMEM((2, SENDERS, RHS, PIECE), F32),
            pltpu.SemaphoreType.DMA((2,)),
            pltpu.SemaphoreType.DMA((2, 32)),
            pltpu.SemaphoreType.DMA((2,)),
            pltpu.SemaphoreType.DMA((2, 2, BLOCKS)),
            pltpu.SemaphoreType.DMA((2,)),
        ],
        compiler_params=pltpu.CompilerParams(
            collective_id=0, has_side_effects=True, vmem_limit_bytes=58 * 1024 * 1024
        ),
        name="peec_pair_products",
    )(currents, right_side, geometry)


def solution(mesh):
    placed = (P(None, ("mirror", "rows")), P(None, ("mirror", "rows", "cols")), P())
    return jax.shard_map(
        on_device,
        mesh=mesh,
        in_specs=placed,
        out_specs=(P(None, ("mirror", "rows", "cols")), P(None, ("mirror", "rows", "cols"))),
        check_vma=False,
    )
```

```python
import functools

import jax
import jax.numpy as jnp
from jax import lax
from jax.experimental import pallas as pl
from jax.experimental.pallas import tpu as pltpu
from jax.sharding import PartitionSpec as P

MESH = pl.DeviceIdType.MESH
F32, BF16 = jnp.float32, jnp.bfloat16
HALF = 65536
RHS = 16
PIECE = 256
SOURCES = 4096
TARGETS = 2048
PIECES = SOURCES // PIECE
BLOCKS = TARGETS // PIECE
TERMS = 32
SQUARE = 2.0**17
ROOT = 2.0**8.5
CHUNK = 256
SENDERS = 16


def split3(value):
    high = value.astype(BF16).astype(F32)
    rest = value - high
    middle = rest.astype(BF16).astype(F32)
    return high, middle, (rest - middle).astype(BF16).astype(F32)


def store_terms(geo, terms, source):
    across = geo[0:1, :] - 0.5
    height = geo[1:2, :] - 0.25
    size = geo[3:4, :]
    own = across * across + height * height + size * size
    xs, ys, qs = split3(across), split3(height), split3(own)
    one = jnp.ones_like(across)
    if source:
        zs = split3(geo[2:3, :] - 2.0)
        rows = [v[i] for v in (xs, ys) for i in (0, 0, 1, 0, 2, 1)]
        rows += [*qs, one, one, one, *zs]
    else:
        rows = [v[i] * (-2.0 * SQUARE) for v in (xs, ys) for i in (0, 1, 0, 2, 0, 1)]
        rows += [one * SQUARE] * 3 + [v * SQUARE for v in qs]
    for k in range(TERMS):
        terms[k : k + 1, :] = rows[k] if k < len(rows) else jnp.zeros_like(across)


def kernel(
    cur_ref, right_ref, geo_ref, res_ref, img_ref,
    a_ref, b_ref, gs_ref, gt_ref, fs_ref, ft_ref, l_ref, r_ref, zb_ref, yb_ref, zt_ref,
    own_ref, j_ref, v_ref, p_ref,
    geo_sem, gather_send, gather_recv, core_send, core_recv, part_send, part_recv,
):
    mirror = lax.axis_index("mirror")
    row = lax.axis_index("rows")
    col = lax.axis_index("cols")
    core = row % 2
    depth = row // 8
    line = (row // 2) % 4
    home = col // 2
    slot = core * 8 + line * 2 + col % 2
    me = mirror * 8 + depth

    barrier = pltpu.get_barrier_semaphore()

    def greet(other):
        pl.semaphore_signal(barrier, inc=1, device_id=other, device_id_type=MESH)

    def greet_source(k, carry):
        other = (k // 8, depth * 8 + (k // 2) % 4 * 2 + core, mirror * 2 + k % 2)

        @pl.when(jnp.logical_not(is_self(*other)))
        def _():
            greet(other)

        return carry

    def is_self(half, other, column):
        return jnp.logical_and(jnp.logical_and(half == mirror, other == row), column == col)

    def greet_part(k, carry):
        @pl.when(k != me)
        def _():
            greet((k // 8, k % 8 * 8 + line * 2 + core, col))

        return carry

    sibling = (mirror, row + 1 - 2 * core, col)
    lax.fori_loop(0, 16, greet_source, 0)
    lax.fori_loop(0, SENDERS, greet_part, 0)
    greet(sibling)

    def source_geo(k, carry):
        start = (depth * 8 + (k // 2) % 4 * 2 + k // 8) * 1024 + (mirror * 2 + k % 2) * PIECE
        pltpu.make_async_copy(
            geo_ref.at[:, pl.ds(pl.multiple_of(start, PIECE), PIECE)],
            gs_ref.at[:, pl.ds(pl.multiple_of(k * PIECE, PIECE), PIECE)],
            geo_sem.at[0],
        ).start()
        return carry

    def target_geo(k, carry):
        start = (k * 8 + line * 2 + core) * 1024 + col * PIECE
        pltpu.make_async_copy(
            geo_ref.at[:, pl.ds(pl.multiple_of(start, PIECE), PIECE)],
            gt_ref.at[:, pl.ds(pl.multiple_of(k * PIECE, PIECE), PIECE)],
            geo_sem.at[1],
        ).start()
        return carry

    lax.fori_loop(0, PIECES, source_geo, 0)
    lax.fori_loop(0, BLOCKS, target_geo, 0)
    own_ref[0] = cur_ref[:, pl.ds(pl.multiple_of(col * PIECE, PIECE), PIECE)]

    def piece_at(which):
        rows = pl.ds(pl.multiple_of(mirror * RHS, RHS), RHS)
        return j_ref.at[which, rows, pl.ds(pl.multiple_of(slot * PIECE, PIECE), PIECE)]

    def gather_copy(which, i):
        return pltpu.make_async_remote_copy(
            src_ref=own_ref.at[which],
            dst_ref=piece_at(which),
            send_sem=gather_send.at[which, i],
            recv_sem=gather_recv.at[which],
            device_id=taker(i),
            device_id_type=MESH,
        )

    def taker(i):
        return home, depth * 8 + (line + i // 4) % 4 * 2 + core, (col + i) % 4

    def gather_start(which):
        def send(i, carry):
            @pl.when(jnp.logical_not(is_self(*taker(i))))
            def _():
                gather_copy(which, i).start()

            return carry

        lax.fori_loop(0, 16, send, 0)

        @pl.when(home == mirror)
        def _():
            pltpu.make_async_copy(own_ref.at[which], piece_at(which), gather_recv.at[which]).start()

    def core_part(which, side):
        return j_ref.at[which, :, pl.ds(pl.multiple_of(side * (SOURCES // 2), SOURCES // 2), SOURCES // 2)]

    def core_copy(which):
        return pltpu.make_async_remote_copy(
            src_ref=core_part(which, core),
            dst_ref=core_part(which, core),
            send_sem=core_send.at[which],
            recv_sem=core_recv.at[which],
            device_id=sibling,
            device_id_type=MESH,
        )

    def gather_wait(which):
        mine = core_part(which, core)
        pltpu.make_async_copy(mine, mine, gather_recv.at[which]).wait()
        core_copy(which).start()
        core_copy(which).wait_recv()

    def part_copy(which, half, block):
        start = pl.multiple_of(block * PIECE, PIECE)
        return pltpu.make_async_remote_copy(
            src_ref=v_ref.at[which, pl.ds(half * RHS, RHS), pl.ds(start, PIECE)],
            dst_ref=p_ref.at[which, me],
            send_sem=part_send.at[which, half, block],
            recv_sem=part_recv.at[which],
            device_id=(half, block * 8 + line * 2 + core, col),
            device_id_type=MESH,
        )

    def part_store(which, block, total):
        start = pl.multiple_of(block * PIECE, PIECE)
        v_ref[which, :, pl.ds(start, PIECE)] = total
        for half in range(2):

            @pl.when(jnp.logical_or(block != depth, mirror != half))
            def _():
                part_copy(which, half, block).start()

        @pl.when(jnp.logical_and(block == depth, mirror == 0))
        def _():
            p_ref[which, me] = total[0:RHS]

        @pl.when(jnp.logical_and(block == depth, mirror == 1))
        def _():
            p_ref[which, me] = total[RHS : 2 * RHS]

    def part_sum(which):
        others = p_ref.at[which, 0 : SENDERS - 1]
        pltpu.make_async_copy(others, others, part_recv.at[which]).wait()
        total = p_ref[which, 0]
        for k in range(1, SENDERS):
            total += p_ref[which, k]
        return total

    pl.semaphore_wait(barrier, jnp.where(home == mirror, 15, 16) + SENDERS)
    gather_start(0)

    pltpu.make_async_copy(gs_ref, gs_ref, geo_sem.at[0]).wait()
    pltpu.make_async_copy(gt_ref, gt_ref, geo_sem.at[1]).wait()
    store_terms(gs_ref, fs_ref, True)
    store_terms(gt_ref, ft_ref, False)
    r_ref[...] = ft_ref[...].astype(BF16)
    zt_ref[0:1, :] = (gt_ref[2:3, :] - 2.0) * ROOT
    zt_ref[1:2, :] = gt_ref[1:2, :]
    l_ref[...] = jnp.transpose(fs_ref[...]).astype(BF16)
    term = lax.broadcasted_iota(jnp.int32, (TERMS, 128), 0)
    pick_z = ((term >= 18) & (term < 21)).astype(BF16)
    pick_y = ((term == 6) | (term == 10) | (term == 11)).astype(BF16)

    def spread(i, carry):
        at = pl.ds(pl.multiple_of(i * 512, 512), 512)
        left = l_ref[at, :]
        zb_ref[at, :] = jnp.dot(left, pick_z, preferred_element_type=F32) * ROOT
        yb_ref[at, :] = (jnp.dot(left, pick_y, preferred_element_type=F32) + 0.25) * (4.0 * SQUARE)
        return carry

    lax.fori_loop(0, SOURCES // 512, spread, 0)

    def make_tile(at, block):
        start = pl.multiple_of(block * PIECE, PIECE)
        rest = jnp.dot(l_ref[at, :], r_ref[:, pl.ds(start, PIECE)], preferred_element_type=F32)
        zb, yb = zb_ref[at, :], yb_ref[at, :]
        near, far = [], []
        for c in range(PIECE // 128):
            lanes = pl.ds(start + c * 128, 128)
            dz = zb - zt_ref[0:1, lanes]
            squared = dz * dz + rest[:, c * 128 : (c + 1) * 128]
            near.append(lax.rsqrt(squared).astype(BF16))
            far.append(lax.rsqrt(squared + yb * zt_ref[1:2, lanes]).astype(BF16))
        near, far = jnp.concatenate(near, 1), jnp.concatenate(far, 1)
        a_ref[at, pl.ds(start, PIECE)] = near
        b_ref[at, pl.ds(start, PIECE)] = far
        return near, far

    def swap(value):
        return jnp.concatenate([value[RHS:], value[:RHS]], 0)

    def build(block):
        def step(i, carry):
            make_tile(pl.ds(pl.multiple_of(i * CHUNK, CHUNK), CHUNK), block)
            return carry

        lax.fori_loop(0, SOURCES // CHUNK, step, 0, unroll=8)

    def build_and_apply(block):
        def step(i, total):
            at = pl.ds(pl.multiple_of(i * CHUNK, CHUNK), CHUNK)
            near, far = make_tile(at, block)
            part = j_ref[0, :, at]
            total += jnp.dot(part, near, preferred_element_type=F32)
            return total + swap(jnp.dot(part, far, preferred_element_type=F32))

        zero = jnp.zeros((2 * RHS, PIECE), F32)
        return lax.fori_loop(0, SOURCES // CHUNK, step, zero, unroll=SOURCES // CHUNK)

    def apply(which, block):
        at = pl.ds(pl.multiple_of(block * PIECE, PIECE), PIECE)
        part = j_ref[which]
        return jnp.dot(part, a_ref[:, at], preferred_element_type=F32) + swap(
            jnp.dot(part, b_ref[:, at], preferred_element_type=F32)
        )

    build(depth)
    gather_wait(0)

    def first(i, carry):
        block = (depth + 1 + i) % BLOCKS
        part_store(0, block, build_and_apply(block))
        return carry

    lax.fori_loop(0, BLOCKS - 1, first, 0)
    part_store(0, depth, apply(0, depth))
    residual = right_ref[...] - part_sum(0)
    res_ref[...] = residual
    own_ref[1] = residual.astype(BF16)

    gather_start(1)
    gather_wait(1)

    def second(i, carry):
        block = (depth + 1 + i) % BLOCKS
        part_store(1, block, apply(1, block))
        return carry

    lax.fori_loop(0, BLOCKS, second, 0)
    img_ref[...] = part_sum(1)

    for which in range(2):

        core_copy(which).wait_send()

        def gathered(i, carry):
            @pl.when(jnp.logical_not(is_self(*taker(i))))
            def _():
                gather_copy(which, i).wait_send()

            return carry

        lax.fori_loop(0, 16, gathered, 0)

        def parted(block, carry):
            for half in range(2):

                @pl.when(jnp.logical_or(block != depth, mirror != half))
                def _():
                    part_copy(which, half, block).wait_send()

            return carry

        lax.fori_loop(0, BLOCKS, parted, 0)


def on_device(currents, right_side, geometry):
    vmem = pl.BlockSpec(memory_space=pltpu.VMEM)
    owned = jax.ShapeDtypeStruct((RHS, PIECE), F32)
    return pl.pallas_call(
        kernel,
        out_shape=(owned, owned),
        in_specs=[vmem, vmem, pl.BlockSpec(memory_space=pl.ANY)],
        out_specs=(vmem, vmem),
        scratch_shapes=[
            pltpu.VMEM((SOURCES, TARGETS), BF16),
            pltpu.VMEM((SOURCES, TARGETS), BF16),
            pltpu.VMEM((4, SOURCES), F32),
            pltpu.VMEM((4, TARGETS), F32),
            pltpu.VMEM((TERMS, SOURCES), F32),
            pltpu.VMEM((TERMS, TARGETS), F32),
            pltpu.VMEM((SOURCES, TERMS), BF16),
            pltpu.VMEM((TERMS, TARGETS), BF16),
            pltpu.VMEM((SOURCES, 128), F32),
            pltpu.VMEM((SOURCES, 128), F32),
            pltpu.VMEM((2, TARGETS), F32),
            pltpu.VMEM((2, RHS, PIECE), BF16),
            pltpu.VMEM((2, 2 * RHS, SOURCES), BF16),
            pltpu.VMEM((2, 2 * RHS, TARGETS), F32),
            pltpu.VMEM((2, SENDERS, RHS, PIECE), F32),
            pltpu.SemaphoreType.DMA((2,)),
            pltpu.SemaphoreType.DMA((2, 16)),
            pltpu.SemaphoreType.DMA((2,)),
            pltpu.SemaphoreType.DMA((2,)),
            pltpu.SemaphoreType.DMA((2,)),
            pltpu.SemaphoreType.DMA((2, 2, BLOCKS)),
            pltpu.SemaphoreType.DMA((2,)),
        ],
        compiler_params=pltpu.CompilerParams(
            collective_id=0, has_side_effects=True, vmem_limit_bytes=58 * 1024 * 1024
        ),
        name="peec_pair_products",
    )(currents, right_side, geometry)


def solution(mesh):
    placed = (P(None, ("mirror", "rows")), P(None, ("mirror", "rows", "cols")), P())
    return jax.shard_map(
        on_device,
        mesh=mesh,
        in_specs=placed,
        out_specs=(P(None, ("mirror", "rows", "cols")), P(None, ("mirror", "rows", "cols"))),
        check_vma=False,
    )
```

```python
import functools

import jax
import jax.numpy as jnp
from jax import lax
from jax.experimental import pallas as pl
from jax.experimental.pallas import tpu as pltpu
from jax.sharding import PartitionSpec as P

MESH = pl.DeviceIdType.MESH
F32, BF16 = jnp.float32, jnp.bfloat16
HALF = 65536
RHS = 16
PIECE = 256
SOURCES = 4096
TARGETS = 2048
PIECES = SOURCES // PIECE
BLOCKS = TARGETS // PIECE
TERMS = 32
SQUARE = 2.0**17
ROOT = 2.0**8.5
CHUNK = 256
SENDERS = 16
FUSED = 3


def split3(value):
    high = value.astype(BF16).astype(F32)
    rest = value - high
    middle = rest.astype(BF16).astype(F32)
    return high, middle, (rest - middle).astype(BF16).astype(F32)


def store_terms(geo, terms, source):
    across = geo[0:1, :] - 0.5
    height = geo[1:2, :] - 0.25
    size = geo[3:4, :]
    own = across * across + height * height + size * size
    xs, ys, qs = split3(across), split3(height), split3(own)
    one = jnp.ones_like(across)
    if source:
        zs = split3(geo[2:3, :] - 2.0)
        rows = [v[i] for v in (xs, ys) for i in (0, 0, 1, 0, 2, 1)]
        rows += [*qs, one, one, one, *zs]
    else:
        rows = [v[i] * (-2.0 * SQUARE) for v in (xs, ys) for i in (0, 1, 0, 2, 0, 1)]
        rows += [one * SQUARE] * 3 + [v * SQUARE for v in qs]
    for k in range(TERMS):
        terms[k : k + 1, :] = rows[k] if k < len(rows) else jnp.zeros_like(across)


def kernel(
    cur_ref, right_ref, geo_ref, res_ref, img_ref,
    a_ref, b_ref, gs_ref, gt_ref, fs_ref, ft_ref, l_ref, r_ref, zb_ref, yb_ref, zt_ref,
    own_ref, j_ref, v_ref, p_ref,
    geo_sem, gather_send, gather_recv, core_send, core_recv, part_send, part_recv,
):
    mirror = lax.axis_index("mirror")
    row = lax.axis_index("rows")
    col = lax.axis_index("cols")
    core = row % 2
    depth = row // 8
    line = (row // 2) % 4
    across = (line + 2) % 4
    home = col // 2
    slot = core * 8 + line * 2 + col % 2
    me = mirror * 8 + depth

    barrier = pltpu.get_barrier_semaphore()

    def greet(other):
        pl.semaphore_signal(barrier, inc=1, device_id=other, device_id_type=MESH)

    def greet_source(k, carry):
        other = (k // 8, depth * 8 + (k // 2) % 4 * 2 + core, mirror * 2 + k % 2)

        @pl.when(jnp.logical_not(is_self(*other)))
        def _():
            greet(other)

        return carry

    def is_self(half, other, column):
        return jnp.logical_and(jnp.logical_and(half == mirror, other == row), column == col)

    def greet_part(k, carry):
        greet((k // 8, k % 8 * 8 + across * 2 + core, col))
        return carry

    sibling = (mirror, row + 1 - 2 * core, col)
    lax.fori_loop(0, 16, greet_source, 0)
    lax.fori_loop(0, SENDERS, greet_part, 0)
    greet(sibling)

    def source_geo(k, carry):
        start = (depth * 8 + (k // 2) % 4 * 2 + k // 8) * 1024 + (mirror * 2 + k % 2) * PIECE
        pltpu.make_async_copy(
            geo_ref.at[:, pl.ds(pl.multiple_of(start, PIECE), PIECE)],
            gs_ref.at[:, pl.ds(pl.multiple_of(k * PIECE, PIECE), PIECE)],
            geo_sem.at[0],
        ).start()
        return carry

    def target_geo(k, carry):
        start = (k * 8 + across * 2 + core) * 1024 + col * PIECE
        pltpu.make_async_copy(
            geo_ref.at[:, pl.ds(pl.multiple_of(start, PIECE), PIECE)],
            gt_ref.at[:, pl.ds(pl.multiple_of(k * PIECE, PIECE), PIECE)],
            geo_sem.at[1],
        ).start()
        return carry

    lax.fori_loop(0, PIECES, source_geo, 0)
    lax.fori_loop(0, BLOCKS, target_geo, 0)
    own_ref[0] = cur_ref[:, pl.ds(pl.multiple_of(col * PIECE, PIECE), PIECE)]

    def piece_at(which):
        rows = pl.ds(pl.multiple_of(mirror * RHS, RHS), RHS)
        return j_ref.at[which, rows, pl.ds(pl.multiple_of(slot * PIECE, PIECE), PIECE)]

    def gather_copy(which, i):
        return pltpu.make_async_remote_copy(
            src_ref=own_ref.at[which],
            dst_ref=piece_at(which),
            send_sem=gather_send.at[which, i],
            recv_sem=gather_recv.at[which],
            device_id=taker(i),
            device_id_type=MESH,
        )

    def taker(i):
        return home, depth * 8 + (line + i // 4) % 4 * 2 + core, (col + i) % 4

    def gather_start(which):
        def send(i, carry):
            @pl.when(jnp.logical_not(is_self(*taker(i))))
            def _():
                gather_copy(which, i).start()

            return carry

        lax.fori_loop(0, 16, send, 0)

        @pl.when(home == mirror)
        def _():
            pltpu.make_async_copy(own_ref.at[which], piece_at(which), gather_recv.at[which]).start()

    def core_part(which, side):
        return j_ref.at[which, :, pl.ds(pl.multiple_of(side * (SOURCES // 2), SOURCES // 2), SOURCES // 2)]

    def core_copy(which):
        return pltpu.make_async_remote_copy(
            src_ref=core_part(which, core),
            dst_ref=core_part(which, core),
            send_sem=core_send.at[which],
            recv_sem=core_recv.at[which],
            device_id=sibling,
            device_id_type=MESH,
        )

    def gather_wait(which):
        mine = core_part(which, core)
        pltpu.make_async_copy(mine, mine, gather_recv.at[which]).wait()
        core_copy(which).start()
        core_copy(which).wait_recv()

    def part_copy(which, half, block):
        start = pl.multiple_of(block * PIECE, PIECE)
        return pltpu.make_async_remote_copy(
            src_ref=v_ref.at[which, pl.ds(half * RHS, RHS), pl.ds(start, PIECE)],
            dst_ref=p_ref.at[which, me],
            send_sem=part_send.at[which, half, block],
            recv_sem=part_recv.at[which],
            device_id=(half, block * 8 + across * 2 + core, col),
            device_id_type=MESH,
        )

    def part_store(which, block, total):
        start = pl.multiple_of(block * PIECE, PIECE)
        v_ref[which, :, pl.ds(start, PIECE)] = total
        for half in range(2):
            part_copy(which, half, block).start()

    def part_sum(which):
        pltpu.make_async_copy(p_ref.at[which], p_ref.at[which], part_recv.at[which]).wait()
        total = p_ref[which, 0]
        for k in range(1, SENDERS):
            total += p_ref[which, k]
        return total

    pl.semaphore_wait(barrier, jnp.where(home == mirror, 15, 16) + SENDERS + 1)
    gather_start(0)

    pltpu.make_async_copy(gs_ref, gs_ref, geo_sem.at[0]).wait()
    pltpu.make_async_copy(gt_ref, gt_ref, geo_sem.at[1]).wait()
    store_terms(gs_ref, fs_ref, True)
    store_terms(gt_ref, ft_ref, False)
    r_ref[...] = ft_ref[...].astype(BF16)
    zt_ref[0:1, :] = (gt_ref[2:3, :] - 2.0) * ROOT
    zt_ref[1:2, :] = gt_ref[1:2, :]
    l_ref[...] = jnp.transpose(fs_ref[...]).astype(BF16)
    term = lax.broadcasted_iota(jnp.int32, (TERMS, 128), 0)
    pick_z = ((term >= 18) & (term < 21)).astype(BF16)
    pick_y = ((term == 6) | (term == 10) | (term == 11)).astype(BF16)

    def spread(i, carry):
        at = pl.ds(pl.multiple_of(i * 512, 512), 512)
        left = l_ref[at, :]
        zb_ref[at, :] = jnp.dot(left, pick_z, preferred_element_type=F32) * ROOT
        yb_ref[at, :] = (jnp.dot(left, pick_y, preferred_element_type=F32) + 0.25) * (4.0 * SQUARE)
        return carry

    lax.fori_loop(0, SOURCES // 512, spread, 0)

    def make_tile(at, block):
        start = pl.multiple_of(block * PIECE, PIECE)
        rest = jnp.dot(l_ref[at, :], r_ref[:, pl.ds(start, PIECE)], preferred_element_type=F32)
        zb, yb = zb_ref[at, :], yb_ref[at, :]
        near, far = [], []
        for c in range(PIECE // 128):
            lanes = pl.ds(start + c * 128, 128)
            dz = zb - zt_ref[0:1, lanes]
            squared = dz * dz + rest[:, c * 128 : (c + 1) * 128]
            near.append(lax.rsqrt(squared).astype(BF16))
            far.append(lax.rsqrt(squared + yb * zt_ref[1:2, lanes]).astype(BF16))
        near, far = jnp.concatenate(near, 1), jnp.concatenate(far, 1)
        a_ref[at, pl.ds(start, PIECE)] = near
        b_ref[at, pl.ds(start, PIECE)] = far
        return near, far

    def swap(value):
        return jnp.concatenate([value[RHS:], value[:RHS]], 0)

    def build(block):
        def step(i, carry):
            make_tile(pl.ds(pl.multiple_of(i * CHUNK, CHUNK), CHUNK), block)
            return carry

        lax.fori_loop(0, SOURCES // CHUNK, step, 0, unroll=SOURCES // CHUNK)

    def build_and_apply(block):
        def step(i, total):
            at = pl.ds(pl.multiple_of(i * CHUNK, CHUNK), CHUNK)
            near, far = make_tile(at, block)
            part = j_ref[0, :, at]
            total += jnp.dot(part, near, preferred_element_type=F32)
            return total + swap(jnp.dot(part, far, preferred_element_type=F32))

        zero = jnp.zeros((2 * RHS, PIECE), F32)
        return lax.fori_loop(0, SOURCES // CHUNK, step, zero, unroll=SOURCES // CHUNK)

    def apply(which, block):
        at = pl.ds(pl.multiple_of(block * PIECE, PIECE), PIECE)
        part = j_ref[which]
        return jnp.dot(part, a_ref[:, at], preferred_element_type=F32) + swap(
            jnp.dot(part, b_ref[:, at], preferred_element_type=F32)
        )

    def block_of(i):
        reach = (i + 1) // 2
        return (depth + 4 + reach * (2 * ((i + 1) % 2) - 1)) % BLOCKS

    def ahead(i, carry):
        build(block_of(i))
        return carry

    lax.fori_loop(FUSED, BLOCKS, ahead, 0)
    gather_wait(0)

    def first(i, carry):
        block = block_of(i)
        part_store(0, block, build_and_apply(block))
        return carry

    lax.fori_loop(0, FUSED, first, 0)

    def rest(i, carry):
        block = block_of(i)
        part_store(0, block, apply(0, block))
        return carry

    lax.fori_loop(FUSED, BLOCKS, rest, 0)
    residual = right_ref[...] - part_sum(0)
    res_ref[...] = residual
    own_ref[1] = residual.astype(BF16)

    gather_start(1)
    gather_wait(1)

    def second(i, carry):
        block = block_of(i)
        part_store(1, block, apply(1, block))
        return carry

    lax.fori_loop(0, BLOCKS, second, 0)
    img_ref[...] = part_sum(1)

    for which in range(2):

        core_copy(which).wait_send()

        def gathered(i, carry):
            @pl.when(jnp.logical_not(is_self(*taker(i))))
            def _():
                gather_copy(which, i).wait_send()

            return carry

        lax.fori_loop(0, 16, gathered, 0)

        def parted(block, carry):
            for half in range(2):
                part_copy(which, half, block).wait_send()

            return carry

        lax.fori_loop(0, BLOCKS, parted, 0)


def on_device(currents, right_side, geometry):
    vmem = pl.BlockSpec(memory_space=pltpu.VMEM)
    owned = jax.ShapeDtypeStruct((RHS, PIECE), F32)
    return pl.pallas_call(
        kernel,
        out_shape=(owned, owned),
        in_specs=[vmem, vmem, pl.BlockSpec(memory_space=pl.ANY)],
        out_specs=(vmem, vmem),
        scratch_shapes=[
            pltpu.VMEM((SOURCES, TARGETS), BF16),
            pltpu.VMEM((SOURCES, TARGETS), BF16),
            pltpu.VMEM((4, SOURCES), F32),
            pltpu.VMEM((4, TARGETS), F32),
            pltpu.VMEM((TERMS, SOURCES), F32),
            pltpu.VMEM((TERMS, TARGETS), F32),
            pltpu.VMEM((SOURCES, TERMS), BF16),
            pltpu.VMEM((TERMS, TARGETS), BF16),
            pltpu.VMEM((SOURCES, 128), F32),
            pltpu.VMEM((SOURCES, 128), F32),
            pltpu.VMEM((2, TARGETS), F32),
            pltpu.VMEM((2, RHS, PIECE), BF16),
            pltpu.VMEM((2, 2 * RHS, SOURCES), BF16),
            pltpu.VMEM((2, 2 * RHS, TARGETS), F32),
            pltpu.VMEM((2, SENDERS, RHS, PIECE), F32),
            pltpu.SemaphoreType.DMA((2,)),
            pltpu.SemaphoreType.DMA((2, 16)),
            pltpu.SemaphoreType.DMA((2,)),
            pltpu.SemaphoreType.DMA((2,)),
            pltpu.SemaphoreType.DMA((2,)),
            pltpu.SemaphoreType.DMA((2, 2, BLOCKS)),
            pltpu.SemaphoreType.DMA((2,)),
        ],
        compiler_params=pltpu.CompilerParams(
            collective_id=0, has_side_effects=True, vmem_limit_bytes=58 * 1024 * 1024
        ),
        name="peec_pair_products",
    )(currents, right_side, geometry)


def solution(mesh):
    placed = (P(None, ("mirror", "rows")), P(None, ("mirror", "rows", "cols")), P())
    return jax.shard_map(
        on_device,
        mesh=mesh,
        in_specs=placed,
        out_specs=(P(None, ("mirror", "rows", "cols")), P(None, ("mirror", "rows", "cols"))),
        check_vma=False,
    )
```

```python
import functools

import jax
import jax.numpy as jnp
from jax import lax
from jax.experimental import pallas as pl
from jax.experimental.pallas import tpu as pltpu
from jax.sharding import PartitionSpec as P

MESH = pl.DeviceIdType.MESH
F32, BF16 = jnp.float32, jnp.bfloat16
HALF = 65536
RHS = 16
PIECE = 256
SOURCES = 4096
TARGETS = 2048
PIECES = SOURCES // PIECE
PART = 2 * PIECE
BLOCKS = TARGETS // PIECE
TERMS = 32
SQUARE = 2.0**17
ROOT = 2.0**8.5
CHUNK = 256
SENDERS = 16
NEAREST = (2, 1, 3, 0)
FUSED = 3


def split3(value):
    high = value.astype(BF16).astype(F32)
    rest = value - high
    middle = rest.astype(BF16).astype(F32)
    return high, middle, (rest - middle).astype(BF16).astype(F32)


def store_terms(geo, terms, source):
    across = geo[0:1, :] - 0.5
    height = geo[1:2, :] - 0.25
    size = geo[3:4, :]
    own = across * across + height * height + size * size
    xs, ys, qs = split3(across), split3(height), split3(own)
    one = jnp.ones_like(across)
    if source:
        zs = split3(geo[2:3, :] - 2.0)
        rows = [v[i] for v in (xs, ys) for i in (0, 0, 1, 0, 2, 1)]
        rows += [*qs, one, one, one, *zs]
    else:
        rows = [v[i] * (-2.0 * SQUARE) for v in (xs, ys) for i in (0, 1, 0, 2, 0, 1)]
        rows += [one * SQUARE] * 3 + [v * SQUARE for v in qs]
    for k in range(TERMS):
        terms[k : k + 1, :] = rows[k] if k < len(rows) else jnp.zeros_like(across)


def kernel(
    cur_ref, right_ref, geo_ref, res_ref, img_ref,
    a_ref, b_ref, gs_ref, gt_ref, fs_ref, ft_ref, l_ref, r_ref, zb_ref, yb_ref, zt_ref,
    own_ref, j_ref, v_ref, p_ref,
    geo_sem, gather_send, gather_recv, core_send, core_recv, part_send, part_recv,
):
    mirror = lax.axis_index("mirror")
    row = lax.axis_index("rows")
    col = lax.axis_index("cols")
    core = row % 2
    depth = row // 8
    line = (row // 2) % 4
    across = (line + 2) % 4
    own_set = (mirror + line) % 2
    home = col // 2
    slot = core * 8 + line * 2 + col % 2
    me = mirror * 8 + depth

    barrier = pltpu.get_barrier_semaphore()

    def greet(other):
        pl.semaphore_signal(barrier, inc=1, device_id=other, device_id_type=MESH)

    def greet_source(k, carry):
        other = (k // 8, depth * 8 + (k // 2) % 4 * 2 + core, own_set * 2 + k % 2)

        @pl.when(jnp.logical_not(is_self(*other)))
        def _():
            greet(other)

        return carry

    def is_self(half, other, column):
        return jnp.logical_and(jnp.logical_and(half == mirror, other == row), column == col)

    def greet_part(k, carry):
        greet((k // 8, k % 8 * 8 + across * 2 + core, col))
        return carry

    sibling = (mirror, row + 1 - 2 * core, col)
    lax.fori_loop(0, 16, greet_source, 0)
    lax.fori_loop(0, SENDERS, greet_part, 0)
    greet(sibling)

    def source_geo(k, carry):
        start = (depth * 8 + (k // 2) % 4 * 2 + k // 8) * 1024 + (own_set * 2 + k % 2) * PIECE
        pltpu.make_async_copy(
            geo_ref.at[:, pl.ds(pl.multiple_of(start, PIECE), PIECE)],
            gs_ref.at[:, pl.ds(pl.multiple_of(k * PIECE, PIECE), PIECE)],
            geo_sem.at[0],
        ).start()
        return carry

    def target_geo(k, carry):
        start = (k * 8 + across * 2 + core) * 1024 + col * PIECE
        pltpu.make_async_copy(
            geo_ref.at[:, pl.ds(pl.multiple_of(start, PIECE), PIECE)],
            gt_ref.at[:, pl.ds(pl.multiple_of(k * PIECE, PIECE), PIECE)],
            geo_sem.at[1],
        ).start()
        return carry

    lax.fori_loop(0, PIECES, source_geo, 0)
    lax.fori_loop(0, BLOCKS, target_geo, 0)
    own_ref[0] = cur_ref[:, pl.ds(pl.multiple_of(col * PIECE, PIECE), PIECE)]

    def piece_at(which):
        rows = pl.ds(pl.multiple_of(mirror * RHS, RHS), RHS)
        return j_ref.at[which, rows, pl.ds(pl.multiple_of(slot * PIECE, PIECE), PIECE)]

    def gather_copy(which, i):
        return pltpu.make_async_remote_copy(
            src_ref=own_ref.at[which],
            dst_ref=piece_at(which),
            send_sem=gather_send.at[which, i],
            recv_sem=gather_recv.at[which, line],
            device_id=taker(i),
            device_id_type=MESH,
        )

    def taker(i):
        other = (line + 2 + i // 4) % 4
        return (home + other) % 2, depth * 8 + other * 2 + core, (col + i) % 4

    def gather_start(which):
        def send(i, carry):
            @pl.when(jnp.logical_not(is_self(*taker(i))))
            def _():
                gather_copy(which, i).start()

            return carry

        lax.fori_loop(0, 16, send, 0)

        @pl.when(home == own_set)
        def _():
            pltpu.make_async_copy(own_ref.at[which], piece_at(which), gather_recv.at[which, line]).start()

    def chunk_at(side, away):
        start = side * (SOURCES // 2) + (line + away) % 4 * PART
        return pl.ds(pl.multiple_of(start, PART), PART)

    def core_copy(which, away):
        part = j_ref.at[which, :, chunk_at(core, away)]
        return pltpu.make_async_remote_copy(
            src_ref=part,
            dst_ref=part,
            send_sem=core_send.at[which, (line + away) % 4],
            recv_sem=core_recv.at[which, (line + away) % 4],
            device_id=sibling,
            device_id_type=MESH,
        )

    def take(which, away):
        part = j_ref.at[which, :, chunk_at(core, away)]
        pltpu.make_async_copy(part, part, gather_recv.at[which, (line + away) % 4]).wait()
        core_copy(which, away).start()

    def take_other(which, away):
        part = j_ref.at[which, :, chunk_at(1 - core, away)]
        pltpu.make_async_copy(part, part, core_recv.at[which, (line + away) % 4]).wait()

    def part_copy(which, half, block):
        start = pl.multiple_of(block * PIECE, PIECE)
        return pltpu.make_async_remote_copy(
            src_ref=v_ref.at[which, pl.ds(half * RHS, RHS), pl.ds(start, PIECE)],
            dst_ref=p_ref.at[which, me],
            send_sem=part_send.at[which, half, block],
            recv_sem=part_recv.at[which],
            device_id=(half, block * 8 + across * 2 + core, col),
            device_id_type=MESH,
        )

    def part_store(which, block, total):
        start = pl.multiple_of(block * PIECE, PIECE)
        v_ref[which, :, pl.ds(start, PIECE)] = total
        for half in range(2):
            part_copy(which, half, block).start()

    def part_sum(which):
        pltpu.make_async_copy(p_ref.at[which], p_ref.at[which], part_recv.at[which]).wait()
        total = p_ref[which, 0]
        for k in range(1, SENDERS):
            total += p_ref[which, k]
        return total

    pl.semaphore_wait(barrier, jnp.where(home == own_set, 15, 16) + SENDERS + 1)
    gather_start(0)

    pltpu.make_async_copy(gs_ref, gs_ref, geo_sem.at[0]).wait()
    pltpu.make_async_copy(gt_ref, gt_ref, geo_sem.at[1]).wait()
    store_terms(gs_ref, fs_ref, True)
    store_terms(gt_ref, ft_ref, False)
    r_ref[...] = ft_ref[...].astype(BF16)
    zt_ref[0:1, :] = (gt_ref[2:3, :] - 2.0) * ROOT
    zt_ref[1:2, :] = gt_ref[1:2, :]
    l_ref[...] = jnp.transpose(fs_ref[...]).astype(BF16)
    term = lax.broadcasted_iota(jnp.int32, (TERMS, 128), 0)
    pick_z = ((term >= 18) & (term < 21)).astype(BF16)
    pick_y = ((term == 6) | (term == 10) | (term == 11)).astype(BF16)

    def spread(i, carry):
        at = pl.ds(pl.multiple_of(i * 512, 512), 512)
        left = l_ref[at, :]
        zb_ref[at, :] = jnp.dot(left, pick_z, preferred_element_type=F32) * ROOT
        yb_ref[at, :] = (jnp.dot(left, pick_y, preferred_element_type=F32) + 0.25) * (4.0 * SQUARE)
        return carry

    lax.fori_loop(0, SOURCES // 512, spread, 0)

    def make_tile(at, block):
        start = pl.multiple_of(block * PIECE, PIECE)
        rest = jnp.dot(l_ref[at, :], r_ref[:, pl.ds(start, PIECE)], preferred_element_type=F32)
        zb, yb = zb_ref[at, :], yb_ref[at, :]
        near, far = [], []
        for c in range(PIECE // 128):
            lanes = pl.ds(start + c * 128, 128)
            dz = zb - zt_ref[0:1, lanes]
            squared = dz * dz + rest[:, c * 128 : (c + 1) * 128]
            near.append(lax.rsqrt(squared).astype(BF16))
            far.append(lax.rsqrt(squared + yb * zt_ref[1:2, lanes]).astype(BF16))
        near, far = jnp.concatenate(near, 1), jnp.concatenate(far, 1)
        a_ref[at, pl.ds(start, PIECE)] = near
        b_ref[at, pl.ds(start, PIECE)] = far
        return near, far

    def swap(value):
        return jnp.concatenate([value[RHS:], value[:RHS]], 0)

    def build(block):
        def step(i, carry):
            make_tile(pl.ds(pl.multiple_of(i * CHUNK, CHUNK), CHUNK), block)
            return carry

        lax.fori_loop(0, SOURCES // CHUNK, step, 0, unroll=SOURCES // CHUNK)

    def build_and_apply(block):
        def step(i, total):
            at = pl.ds(pl.multiple_of(i * CHUNK, CHUNK), CHUNK)
            near, far = make_tile(at, block)
            part = j_ref[0, :, at]
            total += jnp.dot(part, near, preferred_element_type=F32)
            return total + swap(jnp.dot(part, far, preferred_element_type=F32))

        zero = jnp.zeros((2 * RHS, PIECE), F32)
        return lax.fori_loop(0, SOURCES // CHUNK, step, zero, unroll=SOURCES // CHUNK)

    def apply(which, block):
        at = pl.ds(pl.multiple_of(block * PIECE, PIECE), PIECE)
        part = j_ref[which]
        return jnp.dot(part, a_ref[:, at], preferred_element_type=F32) + swap(
            jnp.dot(part, b_ref[:, at], preferred_element_type=F32)
        )

    def block_of(i):
        reach = (i + 1) // 2
        return (depth + 4 + reach * (2 * ((i + 1) % 2) - 1)) % BLOCKS

    def hand_over(i, carry):
        build(block_of(i))

        @pl.when(i == BLOCKS - 2)
        def _():
            for away in NEAREST:
                take(0, away)

        return carry

    lax.fori_loop(FUSED, BLOCKS, hand_over, 0)
    for away in NEAREST:
        take_other(0, away)

    def first(i, carry):
        block = block_of(i)
        part_store(0, block, build_and_apply(block))
        return carry

    lax.fori_loop(0, FUSED, first, 0)

    def rest(i, carry):
        block = block_of(i)
        part_store(0, block, apply(0, block))
        return carry

    lax.fori_loop(FUSED, BLOCKS, rest, 0)
    residual = right_ref[...] - part_sum(0)
    res_ref[...] = residual
    own_ref[1] = residual.astype(BF16)

    gather_start(1)

    def product(chunk, columns):
        part = j_ref[1, :, chunk]
        return jnp.dot(part, a_ref[chunk, columns], preferred_element_type=F32) + swap(
            jnp.dot(part, b_ref[chunk, columns], preferred_element_type=F32)
        )

    def sum_chunk(chunk, fresh):
        def step(i, carry):
            columns = pl.ds(pl.multiple_of(i * PART, PART), PART)
            total = product(chunk, columns)
            v_ref[1, :, columns] = total if fresh else v_ref[1, :, columns] + total
            return carry

        lax.fori_loop(0, TARGETS // PART, step, 0)

    take(1, 2)
    sum_chunk(chunk_at(core, 2), True)
    take(1, 1)
    sum_chunk(chunk_at(core, 1), False)
    take_other(1, 2)
    sum_chunk(chunk_at(1 - core, 2), False)
    take(1, 3)
    sum_chunk(chunk_at(core, 3), False)
    take(1, 0)
    for away in (1, 3, 0):
        take_other(1, away)

    def second(i, carry):
        block = block_of(i)
        columns = pl.ds(pl.multiple_of(block * PIECE, PIECE), PIECE)
        total = v_ref[1, :, columns] + product(chunk_at(core, 0), columns)
        for away in (1, 3, 0):
            total += product(chunk_at(1 - core, away), columns)
        part_store(1, block, total)
        return carry

    lax.fori_loop(0, BLOCKS, second, 0)
    img_ref[...] = part_sum(1)

    for which in range(2):

        for away in NEAREST:
            core_copy(which, away).wait_send()

        def gathered(i, carry):
            @pl.when(jnp.logical_not(is_self(*taker(i))))
            def _():
                gather_copy(which, i).wait_send()

            return carry

        lax.fori_loop(0, 16, gathered, 0)

        def parted(block, carry):
            for half in range(2):
                part_copy(which, half, block).wait_send()

            return carry

        lax.fori_loop(0, BLOCKS, parted, 0)


def settle(residual, image, residual_out, image_out, sems):
    copies = [
        pltpu.make_async_copy(residual, residual_out, sems.at[0]),
        pltpu.make_async_copy(image, image_out, sems.at[1]),
    ]
    for copy in copies:
        copy.start()
    for copy in copies:
        copy.wait()


def on_device(currents, right_side, geometry):
    vmem = pl.BlockSpec(memory_space=pltpu.VMEM)
    owned = jax.ShapeDtypeStruct((RHS, PIECE), F32)
    residual, image = pl.pallas_call(
        kernel,
        out_shape=(owned, owned),
        in_specs=[vmem, vmem, pl.BlockSpec(memory_space=pl.ANY)],
        out_specs=(vmem, vmem),
        scratch_shapes=[
            pltpu.VMEM((SOURCES, TARGETS), BF16),
            pltpu.VMEM((SOURCES, TARGETS), BF16),
            pltpu.VMEM((4, SOURCES), F32),
            pltpu.VMEM((4, TARGETS), F32),
            pltpu.VMEM((TERMS, SOURCES), F32),
            pltpu.VMEM((TERMS, TARGETS), F32),
            pltpu.VMEM((SOURCES, TERMS), BF16),
            pltpu.VMEM((TERMS, TARGETS), BF16),
            pltpu.VMEM((SOURCES, 128), F32),
            pltpu.VMEM((SOURCES, 128), F32),
            pltpu.VMEM((2, TARGETS), F32),
            pltpu.VMEM((2, RHS, PIECE), BF16),
            pltpu.VMEM((2, 2 * RHS, SOURCES), BF16),
            pltpu.VMEM((2, 2 * RHS, TARGETS), F32),
            pltpu.VMEM((2, SENDERS, RHS, PIECE), F32),
            pltpu.SemaphoreType.DMA((2,)),
            pltpu.SemaphoreType.DMA((2, 16)),
            pltpu.SemaphoreType.DMA((2, 4)),
            pltpu.SemaphoreType.DMA((2, 4)),
            pltpu.SemaphoreType.DMA((2, 4)),
            pltpu.SemaphoreType.DMA((2, 2, BLOCKS)),
            pltpu.SemaphoreType.DMA((2,)),
        ],
        compiler_params=pltpu.CompilerParams(
            collective_id=0, has_side_effects=True, vmem_limit_bytes=58 * 1024 * 1024
        ),
        name="peec_pair_products",
    )(currents, right_side, geometry)
    anywhere = pl.BlockSpec(memory_space=pl.ANY)
    return pl.pallas_call(
        settle,
        out_shape=(owned, owned),
        in_specs=[anywhere, anywhere],
        out_specs=(anywhere, anywhere),
        scratch_shapes=[pltpu.SemaphoreType.DMA((2,))],
        name="settle",
    )(residual, image)


def solution(mesh):
    placed = (P(None, ("mirror", "rows")), P(None, ("mirror", "rows", "cols")), P())
    return jax.shard_map(
        on_device,
        mesh=mesh,
        in_specs=placed,
        out_specs=(P(None, ("mirror", "rows", "cols")), P(None, ("mirror", "rows", "cols"))),
        check_vma=False,
    )
```

```python
import functools

import jax
import jax.numpy as jnp
from jax import lax
from jax.experimental import pallas as pl
from jax.experimental.pallas import tpu as pltpu
from jax.sharding import PartitionSpec as P

MESH = pl.DeviceIdType.MESH
F32, BF16 = jnp.float32, jnp.bfloat16
HALF = 65536
RHS = 16
PIECE = 256
SOURCES = 4096
TARGETS = 2048
PIECES = SOURCES // PIECE
PART = 2 * PIECE
BLOCKS = TARGETS // PIECE
TERMS = 32
SQUARE = 2.0**17
ROOT = 2.0**8.5
CHUNK = 256
SENDERS = 16
NEAREST = (2, 1, 3, 0)
FUSED = 3


def split3(value):
    high = value.astype(BF16).astype(F32)
    rest = value - high
    middle = rest.astype(BF16).astype(F32)
    return high, middle, (rest - middle).astype(BF16).astype(F32)


def store_terms(geo, terms, source):
    across = geo[0:1, :] - 0.5
    height = geo[1:2, :] - 0.25
    size = geo[3:4, :]
    own = across * across + height * height + size * size
    xs, ys, qs = split3(across), split3(height), split3(own)
    one = jnp.ones_like(across)
    if source:
        zs = split3(geo[2:3, :] - 2.0)
        rows = [v[i] for v in (xs, ys) for i in (0, 0, 1, 0, 2, 1)]
        rows += [*qs, one, one, one, *zs]
    else:
        rows = [v[i] * (-2.0 * SQUARE) for v in (xs, ys) for i in (0, 1, 0, 2, 0, 1)]
        rows += [one * SQUARE] * 3 + [v * SQUARE for v in qs]
    for k in range(TERMS):
        terms[k : k + 1, :] = rows[k] if k < len(rows) else jnp.zeros_like(across)


def kernel(
    cur_ref, right_ref, geo_ref, res_ref, img_ref,
    a_ref, b_ref, gs_ref, gt_ref, fs_ref, ft_ref, l_ref, r_ref, zb_ref, yb_ref, zt_ref,
    own_ref, j_ref, v_ref, p_ref,
    geo_sem, gather_send, gather_recv, core_send, core_recv, part_send, part_recv,
):
    mirror = lax.axis_index("mirror")
    row = lax.axis_index("rows")
    col = lax.axis_index("cols")
    core = row % 2
    depth = row // 8
    line = (row // 2) % 4
    across = (line + 2) % 4
    own_set = (mirror + line) % 2
    home = col // 2
    slot = core * 8 + line * 2 + col % 2
    me = mirror * 8 + depth

    barrier = pltpu.get_barrier_semaphore()

    def greet(other):
        pl.semaphore_signal(barrier, inc=1, device_id=other, device_id_type=MESH)

    def greet_source(k, carry):
        other = (k // 8, depth * 8 + (k // 2) % 4 * 2 + core, own_set * 2 + k % 2)

        @pl.when(jnp.logical_not(is_self(*other)))
        def _():
            greet(other)

        return carry

    def is_self(half, other, column):
        return jnp.logical_and(jnp.logical_and(half == mirror, other == row), column == col)

    def greet_part(k, carry):
        greet((k // 8, k % 8 * 8 + across * 2 + core, col))
        return carry

    sibling = (mirror, row + 1 - 2 * core, col)
    lax.fori_loop(0, 16, greet_source, 0)
    lax.fori_loop(0, SENDERS, greet_part, 0)
    greet(sibling)

    def source_geo(k, carry):
        start = (depth * 8 + (k // 2) % 4 * 2 + k // 8) * 1024 + (own_set * 2 + k % 2) * PIECE
        pltpu.make_async_copy(
            geo_ref.at[:, pl.ds(pl.multiple_of(start, PIECE), PIECE)],
            gs_ref.at[:, pl.ds(pl.multiple_of(k * PIECE, PIECE), PIECE)],
            geo_sem.at[0],
        ).start()
        return carry

    def target_geo(k, carry):
        start = (k * 8 + across * 2 + core) * 1024 + col * PIECE
        pltpu.make_async_copy(
            geo_ref.at[:, pl.ds(pl.multiple_of(start, PIECE), PIECE)],
            gt_ref.at[:, pl.ds(pl.multiple_of(k * PIECE, PIECE), PIECE)],
            geo_sem.at[1],
        ).start()
        return carry

    lax.fori_loop(0, PIECES, source_geo, 0)
    lax.fori_loop(0, BLOCKS, target_geo, 0)
    own_ref[0] = cur_ref[:, pl.ds(pl.multiple_of(col * PIECE, PIECE), PIECE)]

    def piece_at(which):
        rows = pl.ds(pl.multiple_of(mirror * RHS, RHS), RHS)
        return j_ref.at[which, rows, pl.ds(pl.multiple_of(slot * PIECE, PIECE), PIECE)]

    def gather_copy(which, i):
        return pltpu.make_async_remote_copy(
            src_ref=own_ref.at[which],
            dst_ref=piece_at(which),
            send_sem=gather_send.at[which, i],
            recv_sem=gather_recv.at[which, line],
            device_id=taker(i),
            device_id_type=MESH,
        )

    def taker(i):
        other = (line + 2 + i // 4) % 4
        return (home + other) % 2, depth * 8 + other * 2 + core, (col + i) % 4

    def gather_start(which):
        def send(i, carry):
            @pl.when(jnp.logical_not(is_self(*taker(i))))
            def _():
                gather_copy(which, i).start()

            return carry

        lax.fori_loop(0, 16, send, 0)

        @pl.when(home == own_set)
        def _():
            pltpu.make_async_copy(own_ref.at[which], piece_at(which), gather_recv.at[which, line]).start()

    def chunk_at(side, away):
        start = side * (SOURCES // 2) + (line + away) % 4 * PART
        return pl.ds(pl.multiple_of(start, PART), PART)

    def core_copy(which, away):
        part = j_ref.at[which, :, chunk_at(core, away)]
        return pltpu.make_async_remote_copy(
            src_ref=part,
            dst_ref=part,
            send_sem=core_send.at[which, (line + away) % 4],
            recv_sem=core_recv.at[which, (line + away) % 4],
            device_id=sibling,
            device_id_type=MESH,
        )

    def take(which, away):
        part = j_ref.at[which, :, chunk_at(core, away)]
        pltpu.make_async_copy(part, part, gather_recv.at[which, (line + away) % 4]).wait()
        core_copy(which, away).start()

    def take_other(which, away):
        part = j_ref.at[which, :, chunk_at(1 - core, away)]
        pltpu.make_async_copy(part, part, core_recv.at[which, (line + away) % 4]).wait()

    def part_copy(which, half, block):
        start = pl.multiple_of(block * PIECE, PIECE)
        return pltpu.make_async_remote_copy(
            src_ref=v_ref.at[which, pl.ds(half * RHS, RHS), pl.ds(start, PIECE)],
            dst_ref=p_ref.at[which, me],
            send_sem=part_send.at[which, half, block],
            recv_sem=part_recv.at[which],
            device_id=(half, block * 8 + across * 2 + core, col),
            device_id_type=MESH,
        )

    def part_store(which, block, total):
        start = pl.multiple_of(block * PIECE, PIECE)
        v_ref[which, :, pl.ds(start, PIECE)] = total
        for half in range(2):
            part_copy(which, half, block).start()

    def part_sum(which):
        pltpu.make_async_copy(p_ref.at[which], p_ref.at[which], part_recv.at[which]).wait()
        total = p_ref[which, 0]
        for k in range(1, SENDERS):
            total += p_ref[which, k]
        return total

    pl.semaphore_wait(barrier, jnp.where(home == own_set, 15, 16) + SENDERS + 1)
    gather_start(0)

    pltpu.make_async_copy(gs_ref, gs_ref, geo_sem.at[0]).wait()
    pltpu.make_async_copy(gt_ref, gt_ref, geo_sem.at[1]).wait()
    store_terms(gs_ref, fs_ref, True)
    store_terms(gt_ref, ft_ref, False)
    r_ref[...] = ft_ref[...].astype(BF16)
    zt_ref[0:1, :] = (gt_ref[2:3, :] - 2.0) * ROOT
    zt_ref[1:2, :] = gt_ref[1:2, :]
    l_ref[...] = jnp.transpose(fs_ref[...]).astype(BF16)
    term = lax.broadcasted_iota(jnp.int32, (TERMS, 128), 0)
    pick_z = ((term >= 18) & (term < 21)).astype(BF16)
    pick_y = ((term == 6) | (term == 10) | (term == 11)).astype(BF16)

    def spread(i, carry):
        at = pl.ds(pl.multiple_of(i * 512, 512), 512)
        left = l_ref[at, :]
        zb_ref[at, :] = jnp.dot(left, pick_z, preferred_element_type=F32) * ROOT
        yb_ref[at, :] = (jnp.dot(left, pick_y, preferred_element_type=F32) + 0.25) * (4.0 * SQUARE)
        return carry

    lax.fori_loop(0, SOURCES // 512, spread, 0)

    def make_tile(at, block):
        start = pl.multiple_of(block * PIECE, PIECE)
        rest = jnp.dot(l_ref[at, :], r_ref[:, pl.ds(start, PIECE)], preferred_element_type=F32)
        zb, yb = zb_ref[at, :], yb_ref[at, :]
        near, far = [], []
        for c in range(PIECE // 128):
            lanes = pl.ds(start + c * 128, 128)
            dz = zb - zt_ref[0:1, lanes]
            squared = dz * dz + rest[:, c * 128 : (c + 1) * 128]
            near.append(lax.rsqrt(squared).astype(BF16))
            far.append(lax.rsqrt(squared + yb * zt_ref[1:2, lanes]).astype(BF16))
        near, far = jnp.concatenate(near, 1), jnp.concatenate(far, 1)
        a_ref[at, pl.ds(start, PIECE)] = near
        b_ref[at, pl.ds(start, PIECE)] = far
        return near, far

    def swap(value):
        return jnp.concatenate([value[RHS:], value[:RHS]], 0)

    def build(block):
        def step(i, carry):
            make_tile(pl.ds(pl.multiple_of(i * CHUNK, CHUNK), CHUNK), block)
            return carry

        lax.fori_loop(0, SOURCES // CHUNK, step, 0, unroll=SOURCES // CHUNK)

    def build_and_apply(block):
        def step(i, total):
            at = pl.ds(pl.multiple_of(i * CHUNK, CHUNK), CHUNK)
            near, far = make_tile(at, block)
            part = j_ref[0, :, at]
            total += jnp.dot(part, near, preferred_element_type=F32)
            return total + swap(jnp.dot(part, far, preferred_element_type=F32))

        zero = jnp.zeros((2 * RHS, PIECE), F32)
        return lax.fori_loop(0, SOURCES // CHUNK, step, zero, unroll=SOURCES // CHUNK)

    def apply(which, block):
        at = pl.ds(pl.multiple_of(block * PIECE, PIECE), PIECE)
        part = j_ref[which]
        return jnp.dot(part, a_ref[:, at], preferred_element_type=F32) + swap(
            jnp.dot(part, b_ref[:, at], preferred_element_type=F32)
        )

    def block_of(i):
        reach = (i + 1) // 2
        return (depth + 4 + reach * (2 * ((i + 1) % 2) - 1)) % BLOCKS

    def hand_over(i, carry):
        build(block_of(i))

        @pl.when(i == BLOCKS - 2)
        def _():
            for away in NEAREST:
                take(0, away)

        return carry

    lax.fori_loop(FUSED, BLOCKS, hand_over, 0)
    for away in NEAREST:
        take_other(0, away)

    def first(i, carry):
        block = block_of(i)
        part_store(0, block, build_and_apply(block))
        return carry

    lax.fori_loop(0, FUSED, first, 0)

    def rest(i, carry):
        block = block_of(i)
        part_store(0, block, apply(0, block))
        return carry

    lax.fori_loop(FUSED, BLOCKS, rest, 0)
    residual = right_ref[...] - part_sum(0)
    res_ref[...] = residual
    own_ref[1] = residual.astype(BF16)

    gather_start(1)

    def product(chunk, columns):
        part = j_ref[1, :, chunk]
        return jnp.dot(part, a_ref[chunk, columns], preferred_element_type=F32) + swap(
            jnp.dot(part, b_ref[chunk, columns], preferred_element_type=F32)
        )

    def sum_chunk(chunk, fresh):
        def step(i, carry):
            columns = pl.ds(pl.multiple_of(i * PART, PART), PART)
            total = product(chunk, columns)
            v_ref[1, :, columns] = total if fresh else v_ref[1, :, columns] + total
            return carry

        lax.fori_loop(0, TARGETS // PART, step, 0, unroll=TARGETS // PART)

    take(1, 2)
    sum_chunk(chunk_at(core, 2), True)
    take(1, 1)
    sum_chunk(chunk_at(core, 1), False)
    take_other(1, 2)
    sum_chunk(chunk_at(1 - core, 2), False)
    take(1, 3)
    sum_chunk(chunk_at(core, 3), False)
    take(1, 0)
    for away in (1, 3, 0):
        take_other(1, away)

    def second(i, carry):
        block = block_of(i)
        columns = pl.ds(pl.multiple_of(block * PIECE, PIECE), PIECE)
        total = v_ref[1, :, columns] + product(chunk_at(core, 0), columns)
        for away in (1, 3, 0):
            total += product(chunk_at(1 - core, away), columns)
        part_store(1, block, total)
        return carry

    lax.fori_loop(0, BLOCKS, second, 0, unroll=2)

    for which in range(2):

        for away in NEAREST:
            core_copy(which, away).wait_send()

        def gathered(i, carry):
            @pl.when(jnp.logical_not(is_self(*taker(i))))
            def _():
                gather_copy(which, i).wait_send()

            return carry

        lax.fori_loop(0, 16, gathered, 0)

        def parted(block, carry):
            for half in range(2):
                part_copy(which, half, block).wait_send()

            return carry

        lax.fori_loop(0, BLOCKS, parted, 0)

    img_ref[...] = part_sum(1)


def on_device(currents, right_side, geometry):
    vmem = pl.BlockSpec(memory_space=pltpu.VMEM)
    owned = jax.ShapeDtypeStruct((RHS, PIECE), F32)
    return pl.pallas_call(
        kernel,
        out_shape=(owned, owned),
        in_specs=[vmem, vmem, pl.BlockSpec(memory_space=pl.ANY)],
        out_specs=(vmem, vmem),
        scratch_shapes=[
            pltpu.VMEM((SOURCES, TARGETS), BF16),
            pltpu.VMEM((SOURCES, TARGETS), BF16),
            pltpu.VMEM((4, SOURCES), F32),
            pltpu.VMEM((4, TARGETS), F32),
            pltpu.VMEM((TERMS, SOURCES), F32),
            pltpu.VMEM((TERMS, TARGETS), F32),
            pltpu.VMEM((SOURCES, TERMS), BF16),
            pltpu.VMEM((TERMS, TARGETS), BF16),
            pltpu.VMEM((SOURCES, 128), F32),
            pltpu.VMEM((SOURCES, 128), F32),
            pltpu.VMEM((2, TARGETS), F32),
            pltpu.VMEM((2, RHS, PIECE), BF16),
            pltpu.VMEM((2, 2 * RHS, SOURCES), BF16),
            pltpu.VMEM((2, 2 * RHS, TARGETS), F32),
            pltpu.VMEM((2, SENDERS, RHS, PIECE), F32),
            pltpu.SemaphoreType.DMA((2,)),
            pltpu.SemaphoreType.DMA((2, 16)),
            pltpu.SemaphoreType.DMA((2, 4)),
            pltpu.SemaphoreType.DMA((2, 4)),
            pltpu.SemaphoreType.DMA((2, 4)),
            pltpu.SemaphoreType.DMA((2, 2, BLOCKS)),
            pltpu.SemaphoreType.DMA((2,)),
        ],
        compiler_params=pltpu.CompilerParams(
            collective_id=0, has_side_effects=True, vmem_limit_bytes=58 * 1024 * 1024
        ),
        name="peec_pair_products",
    )(currents, right_side, geometry)


def solution(mesh):
    placed = (P(None, ("mirror", "rows")), P(None, ("mirror", "rows", "cols")), P())
    return jax.shard_map(
        on_device,
        mesh=mesh,
        in_specs=placed,
        out_specs=(P(None, ("mirror", "rows", "cols")), P(None, ("mirror", "rows", "cols"))),
        check_vma=False,
    )
```

```python
import functools

import jax
import jax.numpy as jnp
from jax import lax
from jax.experimental import pallas as pl
from jax.experimental.pallas import tpu as pltpu
from jax.sharding import PartitionSpec as P

MESH = pl.DeviceIdType.MESH
F32, BF16 = jnp.float32, jnp.bfloat16
HALF = 65536
RHS = 16
PIECE = 256
SOURCES = 4096
TARGETS = 2048
PIECES = SOURCES // PIECE
PART = 2 * PIECE
BLOCKS = TARGETS // PIECE
TERMS = 32
SQUARE = 2.0**17
ROOT = 2.0**8.5
CHUNK = 256
SENDERS = 16
NEAREST = (2, 1, 3, 0)
FUSED = 4


def split3(value):
    high = value.astype(BF16).astype(F32)
    rest = value - high
    middle = rest.astype(BF16).astype(F32)
    return high, middle, (rest - middle).astype(BF16).astype(F32)


def store_terms(geo, terms, source):
    across = geo[0:1, :] - 0.5
    height = geo[1:2, :] - 0.25
    size = geo[3:4, :]
    own = across * across + height * height + size * size
    xs, ys, qs = split3(across), split3(height), split3(own)
    one = jnp.ones_like(across)
    if source:
        zs = split3(geo[2:3, :] - 2.0)
        rows = [v[i] for v in (xs, ys) for i in (0, 0, 1, 0, 2, 1)]
        rows += [*qs, one, one, one, *zs]
    else:
        rows = [v[i] * (-2.0 * SQUARE) for v in (xs, ys) for i in (0, 1, 0, 2, 0, 1)]
        rows += [one * SQUARE] * 3 + [v * SQUARE for v in qs]
    for k in range(TERMS):
        terms[k : k + 1, :] = rows[k] if k < len(rows) else jnp.zeros_like(across)


def kernel(
    cur_ref, right_ref, geo_ref, res_ref, img_ref,
    a_ref, b_ref, gs_ref, gt_ref, fs_ref, ft_ref, l_ref, r_ref, zb_ref, yb_ref, zt_ref,
    cur_pair_ref, own_ref, j_ref, v_ref, p_ref,
    geo_sem, gather_send, gather_recv, core_send, core_recv, part_send, part_recv,
):
    mirror = lax.axis_index("mirror")
    row = lax.axis_index("rows")
    col = lax.axis_index("cols")
    core = row % 2
    depth = row // 8
    line = (row // 2) % 4
    across = (line + 2) % 4
    own_set = (mirror + line) % 2
    home = col // 2
    slot = core * 8 + line * 2 + col % 2
    me = mirror * 8 + depth

    barrier = pltpu.get_barrier_semaphore()

    def greet(other):
        pl.semaphore_signal(barrier, inc=1, device_id=other, device_id_type=MESH)

    def greet_source(k, carry):
        other = (k // 8, depth * 8 + (k // 2) % 4 * 2 + core, own_set * 2 + k % 2)

        @pl.when(jnp.logical_not(is_self(*other)))
        def _():
            greet(other)

        return carry

    def is_self(half, other, column):
        return jnp.logical_and(jnp.logical_and(half == mirror, other == row), column == col)

    def greet_part(k, carry):
        greet((k // 8, k % 8 * 8 + across * 2 + core, col))
        return carry

    def along_y(i):
        other = (mirror * 4 + line + i) % 8
        return (other // 4, depth * 8 + other % 4 * 2 + core, col), (other // 4 + other % 4) % 2

    def greet_column(i, carry):
        greet(along_y(i)[0])
        return carry

    sibling = (mirror, row + 1 - 2 * core, col)
    lax.fori_loop(1, 8, greet_column, 0)
    lax.fori_loop(0, 16, greet_source, 0)
    lax.fori_loop(0, SENDERS, greet_part, 0)
    greet(sibling)

    def source_geo(k, carry):
        start = (depth * 8 + (k // 2) % 4 * 2 + k // 8) * 1024 + (own_set * 2 + k % 2) * PIECE
        pltpu.make_async_copy(
            geo_ref.at[:, pl.ds(pl.multiple_of(start, PIECE), PIECE)],
            gs_ref.at[:, pl.ds(pl.multiple_of(k * PIECE, PIECE), PIECE)],
            geo_sem.at[0],
        ).start()
        return carry

    def target_geo(k, carry):
        start = (k * 8 + across * 2 + core) * 1024 + col * PIECE
        pltpu.make_async_copy(
            geo_ref.at[:, pl.ds(pl.multiple_of(start, PIECE), PIECE)],
            gt_ref.at[:, pl.ds(pl.multiple_of(k * PIECE, PIECE), PIECE)],
            geo_sem.at[1],
        ).start()
        return carry

    lax.fori_loop(0, PIECES, source_geo, 0)
    lax.fori_loop(0, BLOCKS, target_geo, 0)
    for half in range(2):
        cur_pair_ref[half] = cur_ref[:, half * PART : (half + 1) * PART]

    def currents_part():
        rows = pl.ds(pl.multiple_of(mirror * RHS, RHS), RHS)
        return j_ref.at[0, rows, pl.ds(pl.multiple_of((core * 4 + line) * PART, PART), PART)]

    def currents_copy(i):
        device, half = along_y(i)
        return pltpu.make_async_remote_copy(
            src_ref=cur_pair_ref.at[half],
            dst_ref=currents_part(),
            send_sem=gather_send.at[0, i],
            recv_sem=gather_recv.at[0, line],
            device_id=device,
            device_id_type=MESH,
        )

    def currents_start():
        def send(i, carry):
            currents_copy(i).start()
            return carry

        lax.fori_loop(1, 8, send, 0)
        pltpu.make_async_copy(cur_pair_ref.at[own_set], currents_part(), gather_recv.at[0, line]).start()

    def piece_at():
        rows = pl.ds(pl.multiple_of(mirror * RHS, RHS), RHS)
        return j_ref.at[1, rows, pl.ds(pl.multiple_of(slot * PIECE, PIECE), PIECE)]

    def gather_copy(i):
        return pltpu.make_async_remote_copy(
            src_ref=own_ref,
            dst_ref=piece_at(),
            send_sem=gather_send.at[1, i],
            recv_sem=gather_recv.at[1, line],
            device_id=taker(i),
            device_id_type=MESH,
        )

    def taker(i):
        other = (line + 2 + i // 4) % 4
        return (home + other) % 2, depth * 8 + other * 2 + core, (col + i) % 4

    def gather_start():
        def send(i, carry):
            @pl.when(jnp.logical_not(is_self(*taker(i))))
            def _():
                gather_copy(i).start()

            return carry

        lax.fori_loop(0, 16, send, 0)

        @pl.when(home == own_set)
        def _():
            pltpu.make_async_copy(own_ref, piece_at(), gather_recv.at[1, line]).start()

    def chunk_at(side, away):
        start = side * (SOURCES // 2) + (line + away) % 4 * PART
        return pl.ds(pl.multiple_of(start, PART), PART)

    def core_copy(which, away):
        part = j_ref.at[which, :, chunk_at(core, away)]
        return pltpu.make_async_remote_copy(
            src_ref=part,
            dst_ref=part,
            send_sem=core_send.at[which, (line + away) % 4],
            recv_sem=core_recv.at[which, (line + away) % 4],
            device_id=sibling,
            device_id_type=MESH,
        )

    def take(which, away):
        part = j_ref.at[which, :, chunk_at(core, away)]
        pltpu.make_async_copy(part, part, gather_recv.at[which, (line + away) % 4]).wait()
        core_copy(which, away).start()

    def take_other(which, away):
        part = j_ref.at[which, :, chunk_at(1 - core, away)]
        pltpu.make_async_copy(part, part, core_recv.at[which, (line + away) % 4]).wait()

    def part_copy(which, half, block):
        start = pl.multiple_of(block * PIECE, PIECE)
        return pltpu.make_async_remote_copy(
            src_ref=v_ref.at[which, pl.ds(half * RHS, RHS), pl.ds(start, PIECE)],
            dst_ref=p_ref.at[which, me],
            send_sem=part_send.at[which, half, block],
            recv_sem=part_recv.at[which],
            device_id=(half, block * 8 + across * 2 + core, col),
            device_id_type=MESH,
        )

    def part_store(which, block, total):
        start = pl.multiple_of(block * PIECE, PIECE)
        v_ref[which, :, pl.ds(start, PIECE)] = total
        for half in range(2):
            part_copy(which, half, block).start()

    def part_sum(which):
        pltpu.make_async_copy(p_ref.at[which], p_ref.at[which], part_recv.at[which]).wait()
        total = p_ref[which, 0]
        for k in range(1, SENDERS):
            total += p_ref[which, k]
        return total

    pl.semaphore_wait(barrier, jnp.where(home == own_set, 15, 16) + SENDERS + 1 + 7)
    currents_start()

    pltpu.make_async_copy(gs_ref, gs_ref, geo_sem.at[0]).wait()
    pltpu.make_async_copy(gt_ref, gt_ref, geo_sem.at[1]).wait()
    store_terms(gs_ref, fs_ref, True)
    store_terms(gt_ref, ft_ref, False)
    r_ref[...] = ft_ref[...].astype(BF16)
    zt_ref[0:1, :] = (gt_ref[2:3, :] - 2.0) * ROOT
    zt_ref[1:2, :] = gt_ref[1:2, :]
    l_ref[...] = jnp.transpose(fs_ref[...]).astype(BF16)
    term = lax.broadcasted_iota(jnp.int32, (TERMS, 128), 0)
    pick_z = ((term >= 18) & (term < 21)).astype(BF16)
    pick_y = ((term == 6) | (term == 10) | (term == 11)).astype(BF16)

    def spread(i, carry):
        at = pl.ds(pl.multiple_of(i * 512, 512), 512)
        left = l_ref[at, :]
        zb_ref[at, :] = jnp.dot(left, pick_z, preferred_element_type=F32) * ROOT
        yb_ref[at, :] = (jnp.dot(left, pick_y, preferred_element_type=F32) + 0.25) * (4.0 * SQUARE)
        return carry

    lax.fori_loop(0, SOURCES // 512, spread, 0)

    def make_tile(at, block):
        start = pl.multiple_of(block * PIECE, PIECE)
        rest = jnp.dot(l_ref[at, :], r_ref[:, pl.ds(start, PIECE)], preferred_element_type=F32)
        zb, yb = zb_ref[at, :], yb_ref[at, :]
        near, far = [], []
        for c in range(PIECE // 128):
            lanes = pl.ds(start + c * 128, 128)
            dz = zb - zt_ref[0:1, lanes]
            squared = dz * dz + rest[:, c * 128 : (c + 1) * 128]
            near.append(lax.rsqrt(squared).astype(BF16))
            far.append(lax.rsqrt(squared + yb * zt_ref[1:2, lanes]).astype(BF16))
        near, far = jnp.concatenate(near, 1), jnp.concatenate(far, 1)
        a_ref[at, pl.ds(start, PIECE)] = near
        b_ref[at, pl.ds(start, PIECE)] = far
        return near, far

    def swap(value):
        return jnp.concatenate([value[RHS:], value[:RHS]], 0)

    def build(block):
        def step(i, carry):
            make_tile(pl.ds(pl.multiple_of(i * CHUNK, CHUNK), CHUNK), block)
            return carry

        lax.fori_loop(0, SOURCES // CHUNK, step, 0, unroll=SOURCES // CHUNK)

    def build_and_apply(block):
        def step(i, total):
            at = pl.ds(pl.multiple_of(i * CHUNK, CHUNK), CHUNK)
            near, far = make_tile(at, block)
            part = j_ref[0, :, at]
            total += jnp.dot(part, near, preferred_element_type=F32)
            return total + swap(jnp.dot(part, far, preferred_element_type=F32))

        zero = jnp.zeros((2 * RHS, PIECE), F32)
        return lax.fori_loop(0, SOURCES // CHUNK, step, zero, unroll=SOURCES // CHUNK)

    def apply(which, block):
        at = pl.ds(pl.multiple_of(block * PIECE, PIECE), PIECE)
        part = j_ref[which]
        return jnp.dot(part, a_ref[:, at], preferred_element_type=F32) + swap(
            jnp.dot(part, b_ref[:, at], preferred_element_type=F32)
        )

    def block_of(i):
        reach = (i + 1) // 2
        return (depth + 4 + reach * (2 * ((i + 1) % 2) - 1)) % BLOCKS

    def hand_over(i, carry):
        build(block_of(i))

        @pl.when(i == BLOCKS - 2)
        def _():
            for away in NEAREST:
                take(0, away)

        return carry

    lax.fori_loop(FUSED, BLOCKS, hand_over, 0)
    for away in NEAREST:
        take_other(0, away)

    def first(i, carry):
        block = block_of(i)
        part_store(0, block, build_and_apply(block))
        return carry

    lax.fori_loop(0, FUSED, first, 0)

    def rest(i, carry):
        block = block_of(i)
        part_store(0, block, apply(0, block))
        return carry

    lax.fori_loop(FUSED, BLOCKS, rest, 0)
    residual = right_ref[...] - part_sum(0)
    res_ref[...] = residual
    own_ref[...] = residual.astype(BF16)

    gather_start()

    def product(chunk, columns):
        part = j_ref[1, :, chunk]
        return jnp.dot(part, a_ref[chunk, columns], preferred_element_type=F32) + swap(
            jnp.dot(part, b_ref[chunk, columns], preferred_element_type=F32)
        )

    def sum_chunk(chunk, fresh):
        def step(i, carry):
            columns = pl.ds(pl.multiple_of(i * PART, PART), PART)
            total = product(chunk, columns)
            v_ref[1, :, columns] = total if fresh else v_ref[1, :, columns] + total
            return carry

        lax.fori_loop(0, TARGETS // PART, step, 0, unroll=TARGETS // PART)

    take(1, 2)
    sum_chunk(chunk_at(core, 2), True)
    take(1, 1)
    sum_chunk(chunk_at(core, 1), False)
    take(1, 3)
    take(1, 0)
    sum_chunk(chunk_at(core, 3), False)
    take_other(1, 2)
    sum_chunk(chunk_at(1 - core, 2), False)
    for away in (1, 3, 0):
        take_other(1, away)

    def second(i, carry):
        block = block_of(i)
        columns = pl.ds(pl.multiple_of(block * PIECE, PIECE), PIECE)
        total = v_ref[1, :, columns] + product(chunk_at(core, 0), columns)
        for away in (1, 3, 0):
            total += product(chunk_at(1 - core, away), columns)
        part_store(1, block, total)
        return carry

    lax.fori_loop(0, BLOCKS, second, 0, unroll=2)

    def currents_left(i, carry):
        currents_copy(i).wait_send()
        return carry

    lax.fori_loop(1, 8, currents_left, 0)

    def gathered(i, carry):
        @pl.when(jnp.logical_not(is_self(*taker(i))))
        def _():
            gather_copy(i).wait_send()

        return carry

    lax.fori_loop(0, 16, gathered, 0)
    for which in range(2):

        for away in NEAREST:
            core_copy(which, away).wait_send()

        def parted(block, carry):
            for half in range(2):
                part_copy(which, half, block).wait_send()

            return carry

        lax.fori_loop(0, BLOCKS, parted, 0)

    img_ref[...] = part_sum(1)


def on_device(currents, right_side, geometry):
    vmem = pl.BlockSpec(memory_space=pltpu.VMEM)
    owned = jax.ShapeDtypeStruct((RHS, PIECE), F32)
    return pl.pallas_call(
        kernel,
        out_shape=(owned, owned),
        in_specs=[vmem, vmem, pl.BlockSpec(memory_space=pl.ANY)],
        out_specs=(vmem, vmem),
        scratch_shapes=[
            pltpu.VMEM((SOURCES, TARGETS), BF16),
            pltpu.VMEM((SOURCES, TARGETS), BF16),
            pltpu.VMEM((4, SOURCES), F32),
            pltpu.VMEM((4, TARGETS), F32),
            pltpu.VMEM((TERMS, SOURCES), F32),
            pltpu.VMEM((TERMS, TARGETS), F32),
            pltpu.VMEM((SOURCES, TERMS), BF16),
            pltpu.VMEM((TERMS, TARGETS), BF16),
            pltpu.VMEM((SOURCES, 128), F32),
            pltpu.VMEM((SOURCES, 128), F32),
            pltpu.VMEM((2, TARGETS), F32),
            pltpu.VMEM((2, RHS, PART), BF16),
            pltpu.VMEM((RHS, PIECE), BF16),
            pltpu.VMEM((2, 2 * RHS, SOURCES), BF16),
            pltpu.VMEM((2, 2 * RHS, TARGETS), F32),
            pltpu.VMEM((2, SENDERS, RHS, PIECE), F32),
            pltpu.SemaphoreType.DMA((2,)),
            pltpu.SemaphoreType.DMA((2, 16)),
            pltpu.SemaphoreType.DMA((2, 4)),
            pltpu.SemaphoreType.DMA((2, 4)),
            pltpu.SemaphoreType.DMA((2, 4)),
            pltpu.SemaphoreType.DMA((2, 2, BLOCKS)),
            pltpu.SemaphoreType.DMA((2,)),
        ],
        compiler_params=pltpu.CompilerParams(
            collective_id=0, has_side_effects=True, vmem_limit_bytes=58 * 1024 * 1024
        ),
        name="peec_pair_products",
    )(currents, right_side, geometry)


def solution(mesh):
    placed = (P(None, ("mirror", "rows")), P(None, ("mirror", "rows", "cols")), P())
    return jax.shard_map(
        on_device,
        mesh=mesh,
        in_specs=placed,
        out_specs=(P(None, ("mirror", "rows", "cols")), P(None, ("mirror", "rows", "cols"))),
        check_vma=False,
    )
```

```python
import functools

import jax
import jax.numpy as jnp
from jax import lax
from jax.experimental import pallas as pl
from jax.experimental.pallas import tpu as pltpu
from jax.sharding import PartitionSpec as P

MESH = pl.DeviceIdType.MESH
F32, BF16 = jnp.float32, jnp.bfloat16
HALF = 65536
RHS = 16
PIECE = 256
SOURCES = 4096
TARGETS = 2048
PIECES = SOURCES // PIECE
PART = 2 * PIECE
BLOCKS = TARGETS // PIECE
TERMS = 32
SQUARE = 2.0**17
ROOT = 2.0**8.5
CHUNK = 256
SENDERS = 16
NEAREST = (2, 1, 3, 0)
FUSED = 4


def split3(value):
    high = value.astype(BF16).astype(F32)
    rest = value - high
    middle = rest.astype(BF16).astype(F32)
    return high, middle, (rest - middle).astype(BF16).astype(F32)


def store_terms(geo, terms, source):
    across = geo[0:1, :] - 0.5
    height = geo[1:2, :] - 0.25
    size = geo[3:4, :]
    own = across * across + height * height + size * size
    xs, ys, qs = split3(across), split3(height), split3(own)
    one = jnp.ones_like(across)
    if source:
        zs = split3(geo[2:3, :] - 2.0)
        rows = [v[i] for v in (xs, ys) for i in (0, 0, 1, 0, 2, 1)]
        rows += [*qs, one, one, one, *zs]
    else:
        rows = [v[i] * (-2.0 * SQUARE) for v in (xs, ys) for i in (0, 1, 0, 2, 0, 1)]
        rows += [one * SQUARE] * 3 + [v * SQUARE for v in qs]
    for k in range(TERMS):
        terms[k : k + 1, :] = rows[k] if k < len(rows) else jnp.zeros_like(across)


def kernel(
    cur_ref, right_ref, geo_ref, res_ref, img_ref,
    a_ref, b_ref, gs_ref, gt_ref, fs_ref, ft_ref, l_ref, r_ref, zb_ref, yb_ref, zt_ref,
    cur_pair_ref, own_ref, j_ref, v_ref, w_ref, p_ref,
    geo_sem, gather_send, gather_recv, core_send, core_recv, part_send, part_recv,
):
    mirror = lax.axis_index("mirror")
    row = lax.axis_index("rows")
    col = lax.axis_index("cols")
    core = row % 2
    depth = row // 8
    line = (row // 2) % 4
    across = (line + 2) % 4
    own_set = (mirror + line) % 2
    home = col // 2
    slot = core * 8 + line * 2 + col % 2
    me = mirror * 8 + depth

    barrier = pltpu.get_barrier_semaphore()

    def greet(other):
        pl.semaphore_signal(barrier, inc=1, device_id=other, device_id_type=MESH)

    def greet_source(k, carry):
        other = (k // 8, depth * 8 + (k // 2) % 4 * 2 + core, own_set * 2 + k % 2)

        @pl.when(jnp.logical_not(is_self(*other)))
        def _():
            greet(other)

        return carry

    def is_self(half, other, column):
        return jnp.logical_and(jnp.logical_and(half == mirror, other == row), column == col)

    def greet_part(k, carry):
        greet((k // 8, k % 8 * 8 + across * 2 + core, col))
        return carry

    def along_y(i):
        other = (mirror * 4 + line + i) % 8
        return (other // 4, depth * 8 + other % 4 * 2 + core, col), (other // 4 + other % 4) % 2

    def greet_column(i, carry):
        greet(along_y(i)[0])
        return carry

    sibling = (mirror, row + 1 - 2 * core, col)
    lax.fori_loop(1, 8, greet_column, 0)
    lax.fori_loop(0, 16, greet_source, 0)
    lax.fori_loop(0, SENDERS, greet_part, 0)
    greet(sibling)

    def source_geo(k, carry):
        start = (depth * 8 + (k // 2) % 4 * 2 + k // 8) * 1024 + (own_set * 2 + k % 2) * PIECE
        pltpu.make_async_copy(
            geo_ref.at[:, pl.ds(pl.multiple_of(start, PIECE), PIECE)],
            gs_ref.at[:, pl.ds(pl.multiple_of(k * PIECE, PIECE), PIECE)],
            geo_sem.at[0],
        ).start()
        return carry

    def target_geo(k, carry):
        start = (k * 8 + across * 2 + core) * 1024 + col * PIECE
        pltpu.make_async_copy(
            geo_ref.at[:, pl.ds(pl.multiple_of(start, PIECE), PIECE)],
            gt_ref.at[:, pl.ds(pl.multiple_of(k * PIECE, PIECE), PIECE)],
            geo_sem.at[1],
        ).start()
        return carry

    lax.fori_loop(0, PIECES, source_geo, 0)
    lax.fori_loop(0, BLOCKS, target_geo, 0)
    for half in range(2):
        cur_pair_ref[half] = cur_ref[:, half * PART : (half + 1) * PART]

    def currents_part():
        rows = pl.ds(pl.multiple_of(mirror * RHS, RHS), RHS)
        return j_ref.at[0, rows, pl.ds(pl.multiple_of((core * 4 + line) * PART, PART), PART)]

    def currents_copy(i):
        device, half = along_y(i)
        return pltpu.make_async_remote_copy(
            src_ref=cur_pair_ref.at[half],
            dst_ref=currents_part(),
            send_sem=gather_send.at[0, i],
            recv_sem=gather_recv.at[0, line],
            device_id=device,
            device_id_type=MESH,
        )

    def currents_start():
        def send(i, carry):
            currents_copy(i).start()
            return carry

        lax.fori_loop(1, 8, send, 0)
        pltpu.make_async_copy(cur_pair_ref.at[own_set], currents_part(), gather_recv.at[0, line]).start()

    def piece_at():
        rows = pl.ds(pl.multiple_of(mirror * RHS, RHS), RHS)
        return j_ref.at[1, rows, pl.ds(pl.multiple_of(slot * PIECE, PIECE), PIECE)]

    def gather_copy(i):
        return pltpu.make_async_remote_copy(
            src_ref=own_ref,
            dst_ref=piece_at(),
            send_sem=gather_send.at[1, i],
            recv_sem=gather_recv.at[1, line],
            device_id=taker(i),
            device_id_type=MESH,
        )

    def taker(i):
        other = (line + 2 + i // 4) % 4
        return (home + other) % 2, depth * 8 + other * 2 + core, (col + i) % 4

    def gather_start():
        def send(i, carry):
            @pl.when(jnp.logical_not(is_self(*taker(i))))
            def _():
                gather_copy(i).start()

            return carry

        lax.fori_loop(0, 16, send, 0)

        @pl.when(home == own_set)
        def _():
            pltpu.make_async_copy(own_ref, piece_at(), gather_recv.at[1, line]).start()

    def chunk_at(side, away):
        start = side * (SOURCES // 2) + (line + away) % 4 * PART
        return pl.ds(pl.multiple_of(start, PART), PART)

    def core_copy(which, away):
        part = j_ref.at[which, :, chunk_at(core, away)]
        return pltpu.make_async_remote_copy(
            src_ref=part,
            dst_ref=part,
            send_sem=core_send.at[which, (line + away) % 4],
            recv_sem=core_recv.at[which, (line + away) % 4],
            device_id=sibling,
            device_id_type=MESH,
        )

    def take(which, away):
        part = j_ref.at[which, :, chunk_at(core, away)]
        pltpu.make_async_copy(part, part, gather_recv.at[which, (line + away) % 4]).wait()
        core_copy(which, away).start()

    def take_other(which, away):
        part = j_ref.at[which, :, chunk_at(1 - core, away)]
        pltpu.make_async_copy(part, part, core_recv.at[which, (line + away) % 4]).wait()

    def part_copy(which, half, block):
        start = pl.multiple_of(block * PIECE, PIECE)
        return pltpu.make_async_remote_copy(
            src_ref=w_ref.at[which, pl.ds(half * RHS, RHS), pl.ds(start, PIECE)],
            dst_ref=p_ref.at[which, me],
            send_sem=part_send.at[which, half, block],
            recv_sem=part_recv.at[which],
            device_id=(half, block * 8 + across * 2 + core, col),
            device_id_type=MESH,
        )

    def part_store(which, block, total):
        start = pl.multiple_of(block * PIECE, PIECE)
        w_ref[which, :, pl.ds(start, PIECE)] = total.astype(BF16)
        for half in range(2):
            part_copy(which, half, block).start()

    def part_sum(which):
        pltpu.make_async_copy(p_ref.at[which], p_ref.at[which], part_recv.at[which]).wait()
        total = p_ref[which, 0].astype(F32)
        for k in range(1, SENDERS):
            total += p_ref[which, k].astype(F32)
        return total

    pl.semaphore_wait(barrier, jnp.where(home == own_set, 15, 16) + SENDERS + 1 + 7)
    currents_start()

    pltpu.make_async_copy(gs_ref, gs_ref, geo_sem.at[0]).wait()
    pltpu.make_async_copy(gt_ref, gt_ref, geo_sem.at[1]).wait()
    store_terms(gs_ref, fs_ref, True)
    store_terms(gt_ref, ft_ref, False)
    r_ref[...] = ft_ref[...].astype(BF16)
    zt_ref[0:1, :] = (gt_ref[2:3, :] - 2.0) * ROOT
    zt_ref[1:2, :] = gt_ref[1:2, :]
    l_ref[...] = jnp.transpose(fs_ref[...]).astype(BF16)
    term = lax.broadcasted_iota(jnp.int32, (TERMS, 128), 0)
    pick_z = ((term >= 18) & (term < 21)).astype(BF16)
    pick_y = ((term == 6) | (term == 10) | (term == 11)).astype(BF16)

    def spread(i, carry):
        at = pl.ds(pl.multiple_of(i * 512, 512), 512)
        left = l_ref[at, :]
        zb_ref[at, :] = jnp.dot(left, pick_z, preferred_element_type=F32) * ROOT
        yb_ref[at, :] = (jnp.dot(left, pick_y, preferred_element_type=F32) + 0.25) * (4.0 * SQUARE)
        return carry

    lax.fori_loop(0, SOURCES // 512, spread, 0)

    def make_tile(at, block):
        start = pl.multiple_of(block * PIECE, PIECE)
        rest = jnp.dot(l_ref[at, :], r_ref[:, pl.ds(start, PIECE)], preferred_element_type=F32)
        zb, yb = zb_ref[at, :], yb_ref[at, :]
        near, far = [], []
        for c in range(PIECE // 128):
            lanes = pl.ds(start + c * 128, 128)
            dz = zb - zt_ref[0:1, lanes]
            squared = dz * dz + rest[:, c * 128 : (c + 1) * 128]
            near.append(lax.rsqrt(squared).astype(BF16))
            far.append(lax.rsqrt(squared + yb * zt_ref[1:2, lanes]).astype(BF16))
        near, far = jnp.concatenate(near, 1), jnp.concatenate(far, 1)
        a_ref[at, pl.ds(start, PIECE)] = near
        b_ref[at, pl.ds(start, PIECE)] = far
        return near, far

    def swap(value):
        return jnp.concatenate([value[RHS:], value[:RHS]], 0)

    def build(block):
        def step(i, carry):
            make_tile(pl.ds(pl.multiple_of(i * CHUNK, CHUNK), CHUNK), block)
            return carry

        lax.fori_loop(0, SOURCES // CHUNK, step, 0, unroll=SOURCES // CHUNK)

    def build_and_apply(block):
        def step(i, total):
            at = pl.ds(pl.multiple_of(i * CHUNK, CHUNK), CHUNK)
            near, far = make_tile(at, block)
            part = j_ref[0, :, at]
            total += jnp.dot(part, near, preferred_element_type=F32)
            return total + swap(jnp.dot(part, far, preferred_element_type=F32))

        zero = jnp.zeros((2 * RHS, PIECE), F32)
        return lax.fori_loop(0, SOURCES // CHUNK, step, zero, unroll=SOURCES // CHUNK)

    def apply(which, block):
        at = pl.ds(pl.multiple_of(block * PIECE, PIECE), PIECE)
        part = j_ref[which]
        return jnp.dot(part, a_ref[:, at], preferred_element_type=F32) + swap(
            jnp.dot(part, b_ref[:, at], preferred_element_type=F32)
        )

    def block_of(i):
        reach = (i + 1) // 2
        return (depth + 4 + reach * (2 * ((i + 1) % 2) - 1)) % BLOCKS

    def hand_over(i, carry):
        build(block_of(i))

        @pl.when(i == BLOCKS - 2)
        def _():
            for away in NEAREST:
                take(0, away)

        return carry

    lax.fori_loop(FUSED, BLOCKS, hand_over, 0)
    for away in NEAREST:
        take_other(0, away)

    def first(i, carry):
        block = block_of(i)
        part_store(0, block, build_and_apply(block))
        return carry

    lax.fori_loop(0, FUSED, first, 0)

    def rest(i, carry):
        block = block_of(i)
        part_store(0, block, apply(0, block))
        return carry

    lax.fori_loop(FUSED, BLOCKS, rest, 0)
    residual = right_ref[...] - part_sum(0)
    res_ref[...] = residual
    own_ref[...] = residual.astype(BF16)

    gather_start()

    def product(chunk, columns):
        part = j_ref[1, :, chunk]
        return jnp.dot(part, a_ref[chunk, columns], preferred_element_type=F32) + swap(
            jnp.dot(part, b_ref[chunk, columns], preferred_element_type=F32)
        )

    def sum_chunk(chunk, fresh):
        def step(i, carry):
            columns = pl.ds(pl.multiple_of(i * PART, PART), PART)
            total = product(chunk, columns)
            v_ref[:, columns] = total if fresh else v_ref[:, columns] + total
            return carry

        lax.fori_loop(0, TARGETS // PART, step, 0, unroll=TARGETS // PART)

    take(1, 2)
    sum_chunk(chunk_at(core, 2), True)
    take(1, 1)
    sum_chunk(chunk_at(core, 1), False)
    take(1, 3)
    take(1, 0)
    sum_chunk(chunk_at(core, 3), False)
    take_other(1, 2)
    sum_chunk(chunk_at(1 - core, 2), False)
    for away in (1, 3, 0):
        take_other(1, away)

    def second(i, carry):
        block = block_of(i)
        columns = pl.ds(pl.multiple_of(block * PIECE, PIECE), PIECE)
        total = v_ref[:, columns] + product(chunk_at(core, 0), columns)
        for away in (1, 3, 0):
            total += product(chunk_at(1 - core, away), columns)
        part_store(1, block, total)
        return carry

    lax.fori_loop(0, BLOCKS, second, 0, unroll=2)

    def currents_left(i, carry):
        currents_copy(i).wait_send()
        return carry

    lax.fori_loop(1, 8, currents_left, 0)

    def gathered(i, carry):
        @pl.when(jnp.logical_not(is_self(*taker(i))))
        def _():
            gather_copy(i).wait_send()

        return carry

    lax.fori_loop(0, 16, gathered, 0)
    for which in range(2):

        for away in NEAREST:
            core_copy(which, away).wait_send()

        def parted(block, carry):
            for half in range(2):
                part_copy(which, half, block).wait_send()

            return carry

        lax.fori_loop(0, BLOCKS, parted, 0)

    img_ref[...] = part_sum(1)


def on_device(currents, right_side, geometry):
    vmem = pl.BlockSpec(memory_space=pltpu.VMEM)
    owned = jax.ShapeDtypeStruct((RHS, PIECE), F32)
    return pl.pallas_call(
        kernel,
        out_shape=(owned, owned),
        in_specs=[vmem, vmem, pl.BlockSpec(memory_space=pl.ANY)],
        out_specs=(vmem, vmem),
        scratch_shapes=[
            pltpu.VMEM((SOURCES, TARGETS), BF16),
            pltpu.VMEM((SOURCES, TARGETS), BF16),
            pltpu.VMEM((4, SOURCES), F32),
            pltpu.VMEM((4, TARGETS), F32),
            pltpu.VMEM((TERMS, SOURCES), F32),
            pltpu.VMEM((TERMS, TARGETS), F32),
            pltpu.VMEM((SOURCES, TERMS), BF16),
            pltpu.VMEM((TERMS, TARGETS), BF16),
            pltpu.VMEM((SOURCES, 128), F32),
            pltpu.VMEM((SOURCES, 128), F32),
            pltpu.VMEM((2, TARGETS), F32),
            pltpu.VMEM((2, RHS, PART), BF16),
            pltpu.VMEM((RHS, PIECE), BF16),
            pltpu.VMEM((2, 2 * RHS, SOURCES), BF16),
            pltpu.VMEM((2 * RHS, TARGETS), F32),
            pltpu.VMEM((2, 2 * RHS, TARGETS), BF16),
            pltpu.VMEM((2, SENDERS, RHS, PIECE), BF16),
            pltpu.SemaphoreType.DMA((2,)),
            pltpu.SemaphoreType.DMA((2, 16)),
            pltpu.SemaphoreType.DMA((2, 4)),
            pltpu.SemaphoreType.DMA((2, 4)),
            pltpu.SemaphoreType.DMA((2, 4)),
            pltpu.SemaphoreType.DMA((2, 2, BLOCKS)),
            pltpu.SemaphoreType.DMA((2,)),
        ],
        compiler_params=pltpu.CompilerParams(
            collective_id=0, has_side_effects=True, vmem_limit_bytes=58 * 1024 * 1024
        ),
        name="peec_pair_products",
    )(currents, right_side, geometry)


def solution(mesh):
    placed = (P(None, ("mirror", "rows")), P(None, ("mirror", "rows", "cols")), P())
    return jax.shard_map(
        on_device,
        mesh=mesh,
        in_specs=placed,
        out_specs=(P(None, ("mirror", "rows", "cols")), P(None, ("mirror", "rows", "cols"))),
        check_vma=False,
    )
```

```python
import functools

import jax
import jax.numpy as jnp
from jax import lax
from jax.experimental import pallas as pl
from jax.experimental.pallas import tpu as pltpu
from jax.sharding import PartitionSpec as P

MESH = pl.DeviceIdType.MESH
F32, BF16 = jnp.float32, jnp.bfloat16
HALF = 65536
RHS = 16
PIECE = 256
SOURCES = 4096
TARGETS = 2048
PIECES = SOURCES // PIECE
PART = 2 * PIECE
BLOCKS = TARGETS // PIECE
TERMS = 32
SQUARE = 2.0**17
ROOT = 2.0**8.5
CHUNK = 256
SENDERS = 16
NEAREST = (2, 1, 3, 0)
FUSED = 3


def split3(value):
    high = value.astype(BF16).astype(F32)
    rest = value - high
    middle = rest.astype(BF16).astype(F32)
    return high, middle, (rest - middle).astype(BF16).astype(F32)


def store_terms(geo, terms, source):
    across = geo[0:1, :] - 0.5
    height = geo[1:2, :] - 0.25
    size = geo[3:4, :]
    own = across * across + height * height + size * size
    xs, ys, qs = split3(across), split3(height), split3(own)
    one = jnp.ones_like(across)
    if source:
        zs = split3(geo[2:3, :] - 2.0)
        rows = [v[i] for v in (xs, ys) for i in (0, 0, 1, 0, 2, 1)]
        rows += [*qs, one, one, one, *zs]
    else:
        rows = [v[i] * (-2.0 * SQUARE) for v in (xs, ys) for i in (0, 1, 0, 2, 0, 1)]
        rows += [one * SQUARE] * 3 + [v * SQUARE for v in qs]
    for k in range(TERMS):
        terms[k : k + 1, :] = rows[k] if k < len(rows) else jnp.zeros_like(across)


def kernel(
    cur_ref, right_ref, geo_ref, out_ref,
    a_ref, b_ref, gs_ref, gt_ref, fs_ref, ft_ref, l_ref, r_ref, zb_ref, yb_ref, zt_ref,
    cur_pair_ref, own_ref, j_ref, v_ref, w_ref, p_ref,
    geo_sem, gather_send, gather_recv, core_send, core_recv, part_send, part_recv,
):
    mirror = lax.axis_index("mirror")
    row = lax.axis_index("rows")
    col = lax.axis_index("cols")
    core = row % 2
    depth = row // 8
    line = (row // 2) % 4
    across = (line + 2) % 4
    own_set = (mirror + line) % 2
    home = col // 2
    slot = core * 8 + line * 2 + col % 2
    me = mirror * 8 + depth

    barrier = pltpu.get_barrier_semaphore()

    def greet(other):
        pl.semaphore_signal(barrier, inc=1, device_id=other, device_id_type=MESH)

    def greet_source(k, carry):
        other = (k // 8, depth * 8 + (k // 2) % 4 * 2 + core, own_set * 2 + k % 2)

        @pl.when(jnp.logical_not(is_self(*other)))
        def _():
            greet(other)

        return carry

    def is_self(half, other, column):
        return jnp.logical_and(jnp.logical_and(half == mirror, other == row), column == col)

    def greet_part(k, carry):
        greet((k // 8, k % 8 * 8 + across * 2 + core, col))
        return carry

    def along_y(i):
        other = (mirror * 4 + line + i) % 8
        return (other // 4, depth * 8 + other % 4 * 2 + core, col), (other // 4 + other % 4) % 2

    def greet_column(i, carry):
        greet(along_y(i)[0])
        return carry

    sibling = (mirror, row + 1 - 2 * core, col)
    lax.fori_loop(1, 8, greet_column, 0)
    lax.fori_loop(0, 16, greet_source, 0)
    lax.fori_loop(0, SENDERS, greet_part, 0)
    greet(sibling)

    def source_geo(k, carry):
        start = (depth * 8 + k % 4 * 2 + k // 4) * 1024 + own_set * PART
        pltpu.make_async_copy(
            geo_ref.at[:, pl.ds(pl.multiple_of(start, PART), PART)],
            gs_ref.at[:, pl.ds(pl.multiple_of(k * PART, PART), PART)],
            geo_sem.at[0],
        ).start()
        return carry

    def target_geo(k, carry):
        start = (k * 8 + across * 2 + core) * 1024 + col * PIECE
        pltpu.make_async_copy(
            geo_ref.at[:, pl.ds(pl.multiple_of(start, PIECE), PIECE)],
            gt_ref.at[:, pl.ds(pl.multiple_of(k * PIECE, PIECE), PIECE)],
            geo_sem.at[1],
        ).start()
        return carry

    lax.fori_loop(0, SOURCES // PART, source_geo, 0)
    lax.fori_loop(0, BLOCKS, target_geo, 0)
    for half in range(2):
        cur_pair_ref[half] = cur_ref[:, half * PART : (half + 1) * PART]

    def currents_part():
        rows = pl.ds(pl.multiple_of(mirror * RHS, RHS), RHS)
        return j_ref.at[0, rows, pl.ds(pl.multiple_of((core * 4 + line) * PART, PART), PART)]

    def currents_copy(i):
        device, half = along_y(i)
        return pltpu.make_async_remote_copy(
            src_ref=cur_pair_ref.at[half],
            dst_ref=currents_part(),
            send_sem=gather_send.at[0, i],
            recv_sem=gather_recv.at[0, line],
            device_id=device,
            device_id_type=MESH,
        )

    def currents_start():
        def send(i, carry):
            currents_copy(i).start()
            return carry

        lax.fori_loop(1, 8, send, 0)
        pltpu.make_async_copy(cur_pair_ref.at[own_set], currents_part(), gather_recv.at[0, line]).start()

    def piece_at():
        rows = pl.ds(pl.multiple_of(mirror * RHS, RHS), RHS)
        return j_ref.at[1, rows, pl.ds(pl.multiple_of(slot * PIECE, PIECE), PIECE)]

    def gather_copy(i):
        return pltpu.make_async_remote_copy(
            src_ref=own_ref,
            dst_ref=piece_at(),
            send_sem=gather_send.at[1, i],
            recv_sem=gather_recv.at[1, line],
            device_id=taker(i),
            device_id_type=MESH,
        )

    def taker(i):
        other = (line + 2 + i // 4) % 4
        return (home + other) % 2, depth * 8 + other * 2 + core, (col + i) % 4

    def gather_start():
        def send(i, carry):
            @pl.when(jnp.logical_not(is_self(*taker(i))))
            def _():
                gather_copy(i).start()

            return carry

        lax.fori_loop(0, 16, send, 0)

        @pl.when(home == own_set)
        def _():
            pltpu.make_async_copy(own_ref, piece_at(), gather_recv.at[1, line]).start()

    def chunk_at(side, away):
        start = side * (SOURCES // 2) + (line + away) % 4 * PART
        return pl.ds(pl.multiple_of(start, PART), PART)

    def core_copy(which, away):
        part = j_ref.at[which, :, chunk_at(core, away)]
        return pltpu.make_async_remote_copy(
            src_ref=part,
            dst_ref=part,
            send_sem=core_send.at[which, (line + away) % 4],
            recv_sem=core_recv.at[which, (line + away) % 4],
            device_id=sibling,
            device_id_type=MESH,
        )

    def take(which, away):
        part = j_ref.at[which, :, chunk_at(core, away)]
        pltpu.make_async_copy(part, part, gather_recv.at[which, (line + away) % 4]).wait()
        core_copy(which, away).start()

    def take_other(which, away):
        part = j_ref.at[which, :, chunk_at(1 - core, away)]
        pltpu.make_async_copy(part, part, core_recv.at[which, (line + away) % 4]).wait()

    def part_copy(which, half, block):
        start = pl.multiple_of(block * PIECE, PIECE)
        return pltpu.make_async_remote_copy(
            src_ref=w_ref.at[which, pl.ds(half * RHS, RHS), pl.ds(start, PIECE)],
            dst_ref=p_ref.at[which, me],
            send_sem=part_send.at[which, half, block],
            recv_sem=part_recv.at[which],
            device_id=(half, block * 8 + across * 2 + core, col),
            device_id_type=MESH,
        )

    def part_store(which, block, total):
        start = pl.multiple_of(block * PIECE, PIECE)
        w_ref[which, :, pl.ds(start, PIECE)] = total.astype(BF16)
        for half in range(2):
            part_copy(which, half, block).start()

    def part_sum(which):
        pltpu.make_async_copy(p_ref.at[which], p_ref.at[which], part_recv.at[which]).wait()
        total = p_ref[which, 0].astype(F32)
        for k in range(1, SENDERS):
            total += p_ref[which, k].astype(F32)
        return total

    pl.semaphore_wait(barrier, jnp.where(home == own_set, 15, 16) + SENDERS + 1 + 7)
    currents_start()

    pltpu.make_async_copy(gs_ref, gs_ref, geo_sem.at[0]).wait()
    pltpu.make_async_copy(gt_ref, gt_ref, geo_sem.at[1]).wait()
    store_terms(gs_ref, fs_ref, True)
    store_terms(gt_ref, ft_ref, False)
    r_ref[...] = ft_ref[...].astype(BF16)
    zt_ref[0:1, :] = (gt_ref[2:3, :] - 2.0) * ROOT
    zt_ref[1:2, :] = gt_ref[1:2, :]
    l_ref[...] = jnp.transpose(fs_ref[...]).astype(BF16)
    term = lax.broadcasted_iota(jnp.int32, (TERMS, 128), 0)
    pick_z = ((term >= 18) & (term < 21)).astype(BF16)
    pick_y = ((term == 6) | (term == 10) | (term == 11)).astype(BF16)

    def spread(i, carry):
        at = pl.ds(pl.multiple_of(i * 512, 512), 512)
        left = l_ref[at, :]
        zb_ref[at, :] = jnp.dot(left, pick_z, preferred_element_type=F32) * ROOT
        yb_ref[at, :] = (jnp.dot(left, pick_y, preferred_element_type=F32) + 0.25) * (4.0 * SQUARE)
        return carry

    lax.fori_loop(0, SOURCES // 512, spread, 0, unroll=SOURCES // 512)

    def make_tile(at, block):
        start = pl.multiple_of(block * PIECE, PIECE)
        rest = jnp.dot(l_ref[at, :], r_ref[:, pl.ds(start, PIECE)], preferred_element_type=F32)
        zb, yb = zb_ref[at, :], yb_ref[at, :]
        near, far = [], []
        for c in range(PIECE // 128):
            lanes = pl.ds(start + c * 128, 128)
            dz = zb - zt_ref[0:1, lanes]
            squared = dz * dz + rest[:, c * 128 : (c + 1) * 128]
            near.append(lax.rsqrt(squared).astype(BF16))
            far.append(lax.rsqrt(squared + yb * zt_ref[1:2, lanes]).astype(BF16))
        near, far = jnp.concatenate(near, 1), jnp.concatenate(far, 1)
        a_ref[at, pl.ds(start, PIECE)] = near
        b_ref[at, pl.ds(start, PIECE)] = far
        return near, far

    def swap(value):
        return jnp.concatenate([value[RHS:], value[:RHS]], 0)

    def build(block):
        def step(i, carry):
            make_tile(pl.ds(pl.multiple_of(i * CHUNK, CHUNK), CHUNK), block)
            return carry

        lax.fori_loop(0, SOURCES // CHUNK, step, 0, unroll=SOURCES // CHUNK)

    def build_and_apply(block):
        def step(i, total):
            at = pl.ds(pl.multiple_of(i * CHUNK, CHUNK), CHUNK)
            near, far = make_tile(at, block)
            part = j_ref[0, :, at]
            total += jnp.dot(part, near, preferred_element_type=F32)
            return total + swap(jnp.dot(part, far, preferred_element_type=F32))

        zero = jnp.zeros((2 * RHS, PIECE), F32)
        return lax.fori_loop(0, SOURCES // CHUNK, step, zero, unroll=SOURCES // CHUNK)

    def apply(which, block):
        at = pl.ds(pl.multiple_of(block * PIECE, PIECE), PIECE)
        part = j_ref[which]
        return jnp.dot(part, a_ref[:, at], preferred_element_type=F32) + swap(
            jnp.dot(part, b_ref[:, at], preferred_element_type=F32)
        )

    def block_of(i):
        reach = (i + 1) // 2
        return (depth + 4 + reach * (2 * ((i + 1) % 2) - 1)) % BLOCKS

    def hand_over(i, carry):
        build(block_of(i))

        @pl.when(i == BLOCKS - 2)
        def _():
            for away in NEAREST:
                take(0, away)

        return carry

    lax.fori_loop(FUSED, BLOCKS, hand_over, 0)
    for away in NEAREST:
        take_other(0, away)

    def first(i, carry):
        block = block_of(i)
        part_store(0, block, build_and_apply(block))
        return carry

    lax.fori_loop(0, FUSED, first, 0)

    def rest(i, carry):
        block = block_of(i)
        part_store(0, block, apply(0, block))
        return carry

    lax.fori_loop(FUSED, BLOCKS, rest, 0)
    residual = right_ref[...] - part_sum(0)
    out_ref[0:RHS] = residual
    own_ref[...] = residual.astype(BF16)

    gather_start()

    def product(chunk, columns):
        part = j_ref[1, :, chunk]
        return jnp.dot(part, a_ref[chunk, columns], preferred_element_type=F32) + swap(
            jnp.dot(part, b_ref[chunk, columns], preferred_element_type=F32)
        )

    def sum_chunk(chunk, fresh):
        def step(i, carry):
            columns = pl.ds(pl.multiple_of(i * PART, PART), PART)
            total = product(chunk, columns)
            v_ref[:, columns] = total if fresh else v_ref[:, columns] + total
            return carry

        lax.fori_loop(0, TARGETS // PART, step, 0, unroll=TARGETS // PART)

    take(1, 2)
    sum_chunk(chunk_at(core, 2), True)
    take(1, 1)
    sum_chunk(chunk_at(core, 1), False)
    take(1, 3)
    take(1, 0)
    sum_chunk(chunk_at(core, 3), False)
    take_other(1, 2)
    sum_chunk(chunk_at(1 - core, 2), False)
    sum_chunk(chunk_at(core, 0), False)
    take_other(1, 1)
    sum_chunk(chunk_at(1 - core, 1), False)
    for away in (3, 0):
        take_other(1, away)

    def second(i, carry):
        block = block_of(i)
        columns = pl.ds(pl.multiple_of(block * PIECE, PIECE), PIECE)
        total = v_ref[:, columns]
        for away in (3, 0):
            total += product(chunk_at(1 - core, away), columns)
        part_store(1, block, total)
        return carry

    lax.fori_loop(0, BLOCKS, second, 0, unroll=4)

    def currents_left(i, carry):
        currents_copy(i).wait_send()
        return carry

    lax.fori_loop(1, 8, currents_left, 0)

    def gathered(i, carry):
        @pl.when(jnp.logical_not(is_self(*taker(i))))
        def _():
            gather_copy(i).wait_send()

        return carry

    lax.fori_loop(0, 16, gathered, 0)
    for which in range(2):

        for away in NEAREST:
            core_copy(which, away).wait_send()

        def parted(block, carry):
            for half in range(2):
                part_copy(which, half, block).wait_send()

            return carry

        lax.fori_loop(0, BLOCKS, parted, 0)

    out_ref[RHS : 2 * RHS] = part_sum(1)


def on_device(currents, right_side, geometry):
    vmem = pl.BlockSpec(memory_space=pltpu.VMEM)
    both = pl.pallas_call(
        kernel,
        out_shape=jax.ShapeDtypeStruct((2 * RHS, PIECE), F32),
        in_specs=[vmem, vmem, pl.BlockSpec(memory_space=pl.ANY)],
        out_specs=vmem,
        scratch_shapes=[
            pltpu.VMEM((SOURCES, TARGETS), BF16),
            pltpu.VMEM((SOURCES, TARGETS), BF16),
            pltpu.VMEM((4, SOURCES), F32),
            pltpu.VMEM((4, TARGETS), F32),
            pltpu.VMEM((TERMS, SOURCES), F32),
            pltpu.VMEM((TERMS, TARGETS), F32),
            pltpu.VMEM((SOURCES, TERMS), BF16),
            pltpu.VMEM((TERMS, TARGETS), BF16),
            pltpu.VMEM((SOURCES, 128), F32),
            pltpu.VMEM((SOURCES, 128), F32),
            pltpu.VMEM((2, TARGETS), F32),
            pltpu.VMEM((2, RHS, PART), BF16),
            pltpu.VMEM((RHS, PIECE), BF16),
            pltpu.VMEM((2, 2 * RHS, SOURCES), BF16),
            pltpu.VMEM((2 * RHS, TARGETS), F32),
            pltpu.VMEM((2, 2 * RHS, TARGETS), BF16),
            pltpu.VMEM((2, SENDERS, RHS, PIECE), BF16),
            pltpu.SemaphoreType.DMA((2,)),
            pltpu.SemaphoreType.DMA((2, 16)),
            pltpu.SemaphoreType.DMA((2, 4)),
            pltpu.SemaphoreType.DMA((2, 4)),
            pltpu.SemaphoreType.DMA((2, 4)),
            pltpu.SemaphoreType.DMA((2, 2, BLOCKS)),
            pltpu.SemaphoreType.DMA((2,)),
        ],
        compiler_params=pltpu.CompilerParams(
            collective_id=0, has_side_effects=True, vmem_limit_bytes=58 * 1024 * 1024
        ),
        name="peec_pair_products",
    )(currents, right_side, geometry)
    return both[:RHS], both[RHS:]


def solution(mesh):
    placed = (P(None, ("mirror", "rows")), P(None, ("mirror", "rows", "cols")), P())
    return jax.shard_map(
        on_device,
        mesh=mesh,
        in_specs=placed,
        out_specs=(P(None, ("mirror", "rows", "cols")), P(None, ("mirror", "rows", "cols"))),
        check_vma=False,
    )
```

```python
import functools

import jax
import jax.numpy as jnp
from jax import lax
from jax.experimental import pallas as pl
from jax.experimental.pallas import tpu as pltpu
from jax.sharding import PartitionSpec as P

MESH = pl.DeviceIdType.MESH
F32, BF16 = jnp.float32, jnp.bfloat16
HALF = 65536
RHS = 16
PIECE = 256
SOURCES = 4096
TARGETS = 2048
PIECES = SOURCES // PIECE
PART = 2 * PIECE
BLOCKS = TARGETS // PIECE
TERMS = 32
SQUARE = 2.0**17
ROOT = 2.0**8.5
CHUNK = 256
SENDERS = 16
NEAREST = (2, 1, 3, 0)
EARLY = 2
FUSED = 3


def split3(value):
    high = value.astype(BF16).astype(F32)
    rest = value - high
    middle = rest.astype(BF16).astype(F32)
    return high, middle, (rest - middle).astype(BF16).astype(F32)


def store_terms(geo, terms, source):
    across = geo[0:1, :] - 0.5
    height = geo[1:2, :] - 0.25
    size = geo[3:4, :]
    own = across * across + height * height + size * size
    xs, ys, qs = split3(across), split3(height), split3(own)
    one = jnp.ones_like(across)
    if source:
        zs = split3(geo[2:3, :] - 2.0)
        rows = [v[i] for v in (xs, ys) for i in (0, 0, 1, 0, 2, 1)]
        rows += [*qs, one, one, one, *zs]
    else:
        rows = [v[i] * (-2.0 * SQUARE) for v in (xs, ys) for i in (0, 1, 0, 2, 0, 1)]
        rows += [one * SQUARE] * 3 + [v * SQUARE for v in qs]
    for k in range(TERMS):
        terms[k : k + 1, :] = rows[k] if k < len(rows) else jnp.zeros_like(across)


def kernel(
    cur_ref, right_ref, geo_ref, out_ref,
    a_ref, b_ref, gs_ref, gt_ref, fs_ref, ft_ref, l_ref, r_ref, zb_ref, yb_ref, zt_ref,
    cur_pair_ref, own_ref, j_ref, v_ref, w_ref, p_ref,
    geo_sem, gather_send, gather_recv, core_send, core_recv, part_send, part_recv,
):
    mirror = lax.axis_index("mirror")
    row = lax.axis_index("rows")
    col = lax.axis_index("cols")
    core = row % 2
    depth = row // 8
    line = (row // 2) % 4
    across = (line + 2) % 4
    own_set = (mirror + line) % 2
    home = col // 2
    slot = core * 8 + line * 2 + col % 2
    me = mirror * 8 + depth

    barrier = pltpu.get_barrier_semaphore()

    def greet(other):
        pl.semaphore_signal(barrier, inc=1, device_id=other, device_id_type=MESH)

    def greet_source(k, carry):
        other = (k // 8, depth * 8 + (k // 2) % 4 * 2 + core, own_set * 2 + k % 2)

        @pl.when(jnp.logical_not(is_self(*other)))
        def _():
            greet(other)

        return carry

    def is_self(half, other, column):
        return jnp.logical_and(jnp.logical_and(half == mirror, other == row), column == col)

    def greet_part(k, carry):
        greet((k // 8, k % 8 * 8 + across * 2 + core, col))
        return carry

    def along_y(i):
        other = (mirror * 4 + line + i) % 8
        return (other // 4, depth * 8 + other % 4 * 2 + core, col), (other // 4 + other % 4) % 2

    def greet_column(i, carry):
        greet(along_y(i)[0])
        return carry

    sibling = (mirror, row + 1 - 2 * core, col)
    lax.fori_loop(1, 8, greet_column, 0)
    lax.fori_loop(0, 16, greet_source, 0)
    lax.fori_loop(0, SENDERS, greet_part, 0)
    greet(sibling)

    def source_geo(k, carry):
        start = (depth * 8 + k % 4 * 2 + k // 4) * 1024 + own_set * PART
        pltpu.make_async_copy(
            geo_ref.at[:, pl.ds(pl.multiple_of(start, PART), PART)],
            gs_ref.at[:, pl.ds(pl.multiple_of(k * PART, PART), PART)],
            geo_sem.at[0],
        ).start()
        return carry

    def target_geo(k, carry):
        start = (k * 8 + across * 2 + core) * 1024 + col * PIECE
        pltpu.make_async_copy(
            geo_ref.at[:, pl.ds(pl.multiple_of(start, PIECE), PIECE)],
            gt_ref.at[:, pl.ds(pl.multiple_of(k * PIECE, PIECE), PIECE)],
            geo_sem.at[1],
        ).start()
        return carry

    lax.fori_loop(0, SOURCES // PART, source_geo, 0)
    lax.fori_loop(0, BLOCKS, target_geo, 0)
    for half in range(2):
        cur_pair_ref[half] = cur_ref[:, half * PART : (half + 1) * PART]

    def currents_part():
        rows = pl.ds(pl.multiple_of(mirror * RHS, RHS), RHS)
        return j_ref.at[0, rows, pl.ds(pl.multiple_of((core * 4 + line) * PART, PART), PART)]

    def currents_copy(i):
        device, half = along_y(i)
        return pltpu.make_async_remote_copy(
            src_ref=cur_pair_ref.at[half],
            dst_ref=currents_part(),
            send_sem=gather_send.at[0, i],
            recv_sem=gather_recv.at[0, line],
            device_id=device,
            device_id_type=MESH,
        )

    def currents_start():
        def send(i, carry):
            currents_copy(i).start()
            return carry

        lax.fori_loop(1, 8, send, 0)
        pltpu.make_async_copy(cur_pair_ref.at[own_set], currents_part(), gather_recv.at[0, line]).start()

    def piece_at():
        rows = pl.ds(pl.multiple_of(mirror * RHS, RHS), RHS)
        return j_ref.at[1, rows, pl.ds(pl.multiple_of(slot * PIECE, PIECE), PIECE)]

    def gather_copy(i):
        return pltpu.make_async_remote_copy(
            src_ref=own_ref,
            dst_ref=piece_at(),
            send_sem=gather_send.at[1, i],
            recv_sem=gather_recv.at[1, line],
            device_id=taker(i),
            device_id_type=MESH,
        )

    def taker(i):
        other = (line + 2 + i // 4) % 4
        return (home + other) % 2, depth * 8 + other * 2 + core, (col + i) % 4

    def gather_start():
        def send(i, carry):
            @pl.when(jnp.logical_not(is_self(*taker(i))))
            def _():
                gather_copy(i).start()

            return carry

        lax.fori_loop(0, 16, send, 0)

        @pl.when(home == own_set)
        def _():
            pltpu.make_async_copy(own_ref, piece_at(), gather_recv.at[1, line]).start()

    def chunk_at(side, away):
        start = side * (SOURCES // 2) + (line + away) % 4 * PART
        return pl.ds(pl.multiple_of(start, PART), PART)

    def core_copy(which, away):
        part = j_ref.at[which, :, chunk_at(core, away)]
        return pltpu.make_async_remote_copy(
            src_ref=part,
            dst_ref=part,
            send_sem=core_send.at[which, (line + away) % 4],
            recv_sem=core_recv.at[which, (line + away) % 4],
            device_id=sibling,
            device_id_type=MESH,
        )

    def take(which, away):
        part = j_ref.at[which, :, chunk_at(core, away)]
        pltpu.make_async_copy(part, part, gather_recv.at[which, (line + away) % 4]).wait()
        core_copy(which, away).start()

    def take_other(which, away):
        part = j_ref.at[which, :, chunk_at(1 - core, away)]
        pltpu.make_async_copy(part, part, core_recv.at[which, (line + away) % 4]).wait()

    def part_copy(which, half, block):
        start = pl.multiple_of(block * PIECE, PIECE)
        return pltpu.make_async_remote_copy(
            src_ref=w_ref.at[which, pl.ds(half * RHS, RHS), pl.ds(start, PIECE)],
            dst_ref=p_ref.at[which, me],
            send_sem=part_send.at[which, half, block],
            recv_sem=part_recv.at[which],
            device_id=(half, block * 8 + across * 2 + core, col),
            device_id_type=MESH,
        )

    def part_store(which, block, total):
        start = pl.multiple_of(block * PIECE, PIECE)
        w_ref[which, :, pl.ds(start, PIECE)] = total.astype(BF16)
        for half in range(2):
            part_copy(which, half, block).start()

    def part_sum(which):
        pltpu.make_async_copy(p_ref.at[which], p_ref.at[which], part_recv.at[which]).wait()
        total = p_ref[which, 0].astype(F32)
        for k in range(1, SENDERS):
            total += p_ref[which, k].astype(F32)
        return total

    pltpu.make_async_copy(gs_ref, gs_ref, geo_sem.at[0]).wait()
    pltpu.make_async_copy(gt_ref, gt_ref, geo_sem.at[1]).wait()
    store_terms(gs_ref, fs_ref, True)
    store_terms(gt_ref, ft_ref, False)
    r_ref[...] = ft_ref[...].astype(BF16)
    zt_ref[0:1, :] = (gt_ref[2:3, :] - 2.0) * ROOT
    zt_ref[1:2, :] = gt_ref[1:2, :]
    l_ref[...] = jnp.transpose(fs_ref[...]).astype(BF16)
    term = lax.broadcasted_iota(jnp.int32, (TERMS, 128), 0)
    pick_z = ((term >= 18) & (term < 21)).astype(BF16)
    pick_y = ((term == 6) | (term == 10) | (term == 11)).astype(BF16)

    def spread(i, carry):
        at = pl.ds(pl.multiple_of(i * 512, 512), 512)
        left = l_ref[at, :]
        zb_ref[at, :] = jnp.dot(left, pick_z, preferred_element_type=F32) * ROOT
        yb_ref[at, :] = (jnp.dot(left, pick_y, preferred_element_type=F32) + 0.25) * (4.0 * SQUARE)
        return carry

    lax.fori_loop(0, SOURCES // 512, spread, 0, unroll=SOURCES // 512)

    def make_tile(at, block):
        start = pl.multiple_of(block * PIECE, PIECE)
        rest = jnp.dot(l_ref[at, :], r_ref[:, pl.ds(start, PIECE)], preferred_element_type=F32)
        zb, yb = zb_ref[at, :], yb_ref[at, :]
        near, far = [], []
        for c in range(PIECE // 128):
            lanes = pl.ds(start + c * 128, 128)
            dz = zb - zt_ref[0:1, lanes]
            squared = dz * dz + rest[:, c * 128 : (c + 1) * 128]
            near.append(lax.rsqrt(squared).astype(BF16))
            far.append(lax.rsqrt(squared + yb * zt_ref[1:2, lanes]).astype(BF16))
        near, far = jnp.concatenate(near, 1), jnp.concatenate(far, 1)
        a_ref[at, pl.ds(start, PIECE)] = near
        b_ref[at, pl.ds(start, PIECE)] = far
        return near, far

    def swap(value):
        return jnp.concatenate([value[RHS:], value[:RHS]], 0)

    def build(block):
        def step(i, carry):
            make_tile(pl.ds(pl.multiple_of(i * CHUNK, CHUNK), CHUNK), block)
            return carry

        lax.fori_loop(0, SOURCES // CHUNK, step, 0, unroll=SOURCES // CHUNK)

    def build_and_apply(block):
        def step(i, total):
            at = pl.ds(pl.multiple_of(i * CHUNK, CHUNK), CHUNK)
            near, far = make_tile(at, block)
            part = j_ref[0, :, at]
            total += jnp.dot(part, near, preferred_element_type=F32)
            return total + swap(jnp.dot(part, far, preferred_element_type=F32))

        zero = jnp.zeros((2 * RHS, PIECE), F32)
        return lax.fori_loop(0, SOURCES // CHUNK, step, zero, unroll=SOURCES // CHUNK)

    def apply(which, block):
        at = pl.ds(pl.multiple_of(block * PIECE, PIECE), PIECE)
        part = j_ref[which]
        return jnp.dot(part, a_ref[:, at], preferred_element_type=F32) + swap(
            jnp.dot(part, b_ref[:, at], preferred_element_type=F32)
        )

    def block_of(i):
        reach = (i + 1) // 2
        return (depth + 4 + reach * (2 * ((i + 1) % 2) - 1)) % BLOCKS

    def hand_over(i, carry):
        build(block_of(i))

        @pl.when(i == BLOCKS - 2)
        def _():
            for away in NEAREST:
                take(0, away)

        return carry

    def ahead(i, carry):
        build(block_of(i))
        return carry

    lax.fori_loop(FUSED, FUSED + EARLY, ahead, 0)
    pl.semaphore_wait(barrier, jnp.where(home == own_set, 15, 16) + SENDERS + 1 + 7)
    currents_start()
    lax.fori_loop(FUSED + EARLY, BLOCKS, hand_over, 0)
    for away in NEAREST:
        take_other(0, away)

    def first(i, carry):
        block = block_of(i)
        part_store(0, block, build_and_apply(block))
        return carry

    lax.fori_loop(0, FUSED, first, 0)

    def rest(i, carry):
        block = block_of(i)
        part_store(0, block, apply(0, block))
        return carry

    lax.fori_loop(FUSED, BLOCKS, rest, 0)
    residual = right_ref[...] - part_sum(0)
    out_ref[0:RHS] = residual
    own_ref[...] = residual.astype(BF16)

    gather_start()

    def product(chunk, columns):
        part = j_ref[1, :, chunk]
        return jnp.dot(part, a_ref[chunk, columns], preferred_element_type=F32) + swap(
            jnp.dot(part, b_ref[chunk, columns], preferred_element_type=F32)
        )

    def sum_chunk(chunk, fresh):
        def step(i, carry):
            columns = pl.ds(pl.multiple_of(i * PART, PART), PART)
            total = product(chunk, columns)
            v_ref[:, columns] = total if fresh else v_ref[:, columns] + total
            return carry

        lax.fori_loop(0, TARGETS // PART, step, 0, unroll=TARGETS // PART)

    take(1, 2)
    sum_chunk(chunk_at(core, 2), True)
    take(1, 1)
    sum_chunk(chunk_at(core, 1), False)
    take(1, 3)
    take(1, 0)
    sum_chunk(chunk_at(core, 3), False)
    take_other(1, 2)
    sum_chunk(chunk_at(1 - core, 2), False)
    sum_chunk(chunk_at(core, 0), False)
    take_other(1, 1)
    sum_chunk(chunk_at(1 - core, 1), False)
    for away in (3, 0):
        take_other(1, away)

    def second(i, carry):
        block = block_of(i)
        columns = pl.ds(pl.multiple_of(block * PIECE, PIECE), PIECE)
        total = v_ref[:, columns]
        for away in (3, 0):
            total += product(chunk_at(1 - core, away), columns)
        part_store(1, block, total)
        return carry

    lax.fori_loop(0, BLOCKS, second, 0, unroll=4)

    def currents_left(i, carry):
        currents_copy(i).wait_send()
        return carry

    lax.fori_loop(1, 8, currents_left, 0)

    def gathered(i, carry):
        @pl.when(jnp.logical_not(is_self(*taker(i))))
        def _():
            gather_copy(i).wait_send()

        return carry

    lax.fori_loop(0, 16, gathered, 0)
    for which in range(2):

        for away in NEAREST:
            core_copy(which, away).wait_send()

        def parted(block, carry):
            for half in range(2):
                part_copy(which, half, block).wait_send()

            return carry

        lax.fori_loop(0, BLOCKS, parted, 0)

    out_ref[RHS : 2 * RHS] = part_sum(1)


def on_device(currents, right_side, geometry):
    vmem = pl.BlockSpec(memory_space=pltpu.VMEM)
    both = pl.pallas_call(
        kernel,
        out_shape=jax.ShapeDtypeStruct((2 * RHS, PIECE), F32),
        in_specs=[vmem, vmem, pl.BlockSpec(memory_space=pl.ANY)],
        out_specs=vmem,
        scratch_shapes=[
            pltpu.VMEM((SOURCES, TARGETS), BF16),
            pltpu.VMEM((SOURCES, TARGETS), BF16),
            pltpu.VMEM((4, SOURCES), F32),
            pltpu.VMEM((4, TARGETS), F32),
            pltpu.VMEM((TERMS, SOURCES), F32),
            pltpu.VMEM((TERMS, TARGETS), F32),
            pltpu.VMEM((SOURCES, TERMS), BF16),
            pltpu.VMEM((TERMS, TARGETS), BF16),
            pltpu.VMEM((SOURCES, 128), F32),
            pltpu.VMEM((SOURCES, 128), F32),
            pltpu.VMEM((2, TARGETS), F32),
            pltpu.VMEM((2, RHS, PART), BF16),
            pltpu.VMEM((RHS, PIECE), BF16),
            pltpu.VMEM((2, 2 * RHS, SOURCES), BF16),
            pltpu.VMEM((2 * RHS, TARGETS), F32),
            pltpu.VMEM((2, 2 * RHS, TARGETS), BF16),
            pltpu.VMEM((2, SENDERS, RHS, PIECE), BF16),
            pltpu.SemaphoreType.DMA((2,)),
            pltpu.SemaphoreType.DMA((2, 16)),
            pltpu.SemaphoreType.DMA((2, 4)),
            pltpu.SemaphoreType.DMA((2, 4)),
            pltpu.SemaphoreType.DMA((2, 4)),
            pltpu.SemaphoreType.DMA((2, 2, BLOCKS)),
            pltpu.SemaphoreType.DMA((2,)),
        ],
        compiler_params=pltpu.CompilerParams(
            collective_id=0, has_side_effects=True, vmem_limit_bytes=58 * 1024 * 1024
        ),
        name="peec_pair_products",
    )(currents, right_side, geometry)
    return both[:RHS], both[RHS:]


def solution(mesh):
    placed = (P(None, ("mirror", "rows")), P(None, ("mirror", "rows", "cols")), P())
    return jax.shard_map(
        on_device,
        mesh=mesh,
        in_specs=placed,
        out_specs=(P(None, ("mirror", "rows", "cols")), P(None, ("mirror", "rows", "cols"))),
        check_vma=False,
    )
```

```python
import functools

import jax
import jax.numpy as jnp
from jax import lax
from jax.experimental import pallas as pl
from jax.experimental.pallas import tpu as pltpu
from jax.sharding import PartitionSpec as P

MESH = pl.DeviceIdType.MESH
F32, BF16 = jnp.float32, jnp.bfloat16
HALF = 65536
RHS = 16
PIECE = 256
SOURCES = 4096
TARGETS = 2048
PIECES = SOURCES // PIECE
PART = 2 * PIECE
BLOCKS = TARGETS // PIECE
TERMS = 32
SQUARE = 2.0**17
ROOT = 2.0**8.5
CHUNK = 256
SENDERS = 16
NEAREST = (2, 1, 3, 0)
FUSED = 3


def split3(value):
    high = value.astype(BF16).astype(F32)
    rest = value - high
    middle = rest.astype(BF16).astype(F32)
    return high, middle, (rest - middle).astype(BF16).astype(F32)


def store_terms(geo, terms, source):
    across = geo[0:1, :] - 0.5
    height = geo[1:2, :] - 0.25
    size = geo[3:4, :]
    own = across * across + height * height + size * size
    xs, ys, qs = split3(across), split3(height), split3(own)
    one = jnp.ones_like(across)
    if source:
        zs = split3(geo[2:3, :] - 2.0)
        rows = [v[i] for v in (xs, ys) for i in (0, 0, 1, 0, 2, 1)]
        rows += [*qs, one, one, one, *zs]
    else:
        rows = [v[i] * (-2.0 * SQUARE) for v in (xs, ys) for i in (0, 1, 0, 2, 0, 1)]
        rows += [one * SQUARE] * 3 + [v * SQUARE for v in qs]
    for k in range(TERMS):
        terms[k : k + 1, :] = rows[k] if k < len(rows) else jnp.zeros_like(across)


def kernel(
    cur_ref, right_ref, geo_ref, out_ref,
    a_ref, b_ref, gs_ref, gt_ref, fs_ref, ft_ref, l_ref, r_ref, zb_ref, yb_ref, zt_ref,
    cur_pair_ref, own_ref, j_ref, v_ref, w_ref, p_ref,
    geo_sem, gather_send, gather_recv, core_send, core_recv, part_send, part_recv,
):
    mirror = lax.axis_index("mirror")
    row = lax.axis_index("rows")
    col = lax.axis_index("cols")
    core = row % 2
    depth = row // 8
    line = (row // 2) % 4
    across = (line + 2) % 4
    own_set = (mirror + line) % 2
    home = col // 2
    slot = core * 8 + line * 2 + col % 2
    me = mirror * 8 + depth

    barrier = pltpu.get_barrier_semaphore()

    def greet(other):
        pl.semaphore_signal(barrier, inc=1, device_id=other, device_id_type=MESH)

    def greet_source(k, carry):
        other = (k // 8, depth * 8 + (k // 2) % 4 * 2 + core, own_set * 2 + k % 2)

        @pl.when(jnp.logical_not(is_self(*other)))
        def _():
            greet(other)

        return carry

    def is_self(half, other, column):
        return jnp.logical_and(jnp.logical_and(half == mirror, other == row), column == col)

    def greet_part(k, carry):
        greet((k // 8, k % 8 * 8 + across * 2 + core, col))
        return carry

    def along_y(i):
        other = (mirror * 4 + line + i) % 8
        return (other // 4, depth * 8 + other % 4 * 2 + core, col), (other // 4 + other % 4) % 2

    def greet_column(i, carry):
        greet(along_y(i)[0])
        return carry

    sibling = (mirror, row + 1 - 2 * core, col)
    lax.fori_loop(1, 8, greet_column, 0)
    lax.fori_loop(0, 16, greet_source, 0)
    lax.fori_loop(0, SENDERS, greet_part, 0)
    greet(sibling)

    def source_geo(k, carry):
        start = (depth * 8 + k % 4 * 2 + k // 4) * 1024 + own_set * PART
        pltpu.make_async_copy(
            geo_ref.at[:, pl.ds(pl.multiple_of(start, PART), PART)],
            gs_ref.at[:, pl.ds(pl.multiple_of(k * PART, PART), PART)],
            geo_sem.at[0],
        ).start()
        return carry

    def target_geo(k, carry):
        start = (k * 8 + across * 2 + core) * 1024 + col * PIECE
        pltpu.make_async_copy(
            geo_ref.at[:, pl.ds(pl.multiple_of(start, PIECE), PIECE)],
            gt_ref.at[:, pl.ds(pl.multiple_of(k * PIECE, PIECE), PIECE)],
            geo_sem.at[1],
        ).start()
        return carry

    lax.fori_loop(0, SOURCES // PART, source_geo, 0)
    lax.fori_loop(0, BLOCKS, target_geo, 0)
    for half in range(2):
        cur_pair_ref[half] = cur_ref[:, half * PART : (half + 1) * PART]

    def currents_part():
        rows = pl.ds(pl.multiple_of(mirror * RHS, RHS), RHS)
        return j_ref.at[0, rows, pl.ds(pl.multiple_of((core * 4 + line) * PART, PART), PART)]

    def currents_copy(i):
        device, half = along_y(i)
        return pltpu.make_async_remote_copy(
            src_ref=cur_pair_ref.at[half],
            dst_ref=currents_part(),
            send_sem=gather_send.at[0, i],
            recv_sem=gather_recv.at[0, line],
            device_id=device,
            device_id_type=MESH,
        )

    def currents_start():
        def send(i, carry):
            currents_copy(i).start()
            return carry

        lax.fori_loop(1, 8, send, 0)
        pltpu.make_async_copy(cur_pair_ref.at[own_set], currents_part(), gather_recv.at[0, line]).start()

    def piece_at():
        rows = pl.ds(pl.multiple_of(mirror * RHS, RHS), RHS)
        return j_ref.at[1, rows, pl.ds(pl.multiple_of(slot * PIECE, PIECE), PIECE)]

    def gather_copy(i):
        return pltpu.make_async_remote_copy(
            src_ref=own_ref,
            dst_ref=piece_at(),
            send_sem=gather_send.at[1, i],
            recv_sem=gather_recv.at[1, line],
            device_id=taker(i),
            device_id_type=MESH,
        )

    def taker(i):
        other = (line + 2 + i // 4) % 4
        return (home + other) % 2, depth * 8 + other * 2 + core, (col + i) % 4

    def gather_start():
        def send(i, carry):
            @pl.when(jnp.logical_not(is_self(*taker(i))))
            def _():
                gather_copy(i).start()

            return carry

        lax.fori_loop(0, 16, send, 0)

        @pl.when(home == own_set)
        def _():
            pltpu.make_async_copy(own_ref, piece_at(), gather_recv.at[1, line]).start()

    def chunk_at(side, away):
        start = side * (SOURCES // 2) + (line + away) % 4 * PART
        return pl.ds(pl.multiple_of(start, PART), PART)

    def core_copy(which, away):
        part = j_ref.at[which, :, chunk_at(core, away)]
        return pltpu.make_async_remote_copy(
            src_ref=part,
            dst_ref=part,
            send_sem=core_send.at[which, (line + away) % 4],
            recv_sem=core_recv.at[which, (line + away) % 4],
            device_id=sibling,
            device_id_type=MESH,
        )

    def take(which, away):
        part = j_ref.at[which, :, chunk_at(core, away)]
        pltpu.make_async_copy(part, part, gather_recv.at[which, (line + away) % 4]).wait()
        core_copy(which, away).start()

    def take_other(which, away):
        part = j_ref.at[which, :, chunk_at(1 - core, away)]
        pltpu.make_async_copy(part, part, core_recv.at[which, (line + away) % 4]).wait()

    def part_copy(which, half, block):
        start = pl.multiple_of(block * PIECE, PIECE)
        return pltpu.make_async_remote_copy(
            src_ref=w_ref.at[which, pl.ds(half * RHS, RHS), pl.ds(start, PIECE)],
            dst_ref=p_ref.at[which, me],
            send_sem=part_send.at[which, half, block],
            recv_sem=part_recv.at[which],
            device_id=(half, block * 8 + across * 2 + core, col),
            device_id_type=MESH,
        )

    def part_store(which, block, total):
        start = pl.multiple_of(block * PIECE, PIECE)
        w_ref[which, :, pl.ds(start, PIECE)] = total.astype(BF16)
        for half in range(2):
            part_copy(which, half, block).start()

    def part_sum(which):
        pltpu.make_async_copy(p_ref.at[which], p_ref.at[which], part_recv.at[which]).wait()
        total = p_ref[which, 0].astype(F32)
        for k in range(1, SENDERS):
            total += p_ref[which, k].astype(F32)
        return total

    pltpu.make_async_copy(gs_ref, gs_ref, geo_sem.at[0]).wait()
    pltpu.make_async_copy(gt_ref, gt_ref, geo_sem.at[1]).wait()
    store_terms(gs_ref, fs_ref, True)
    store_terms(gt_ref, ft_ref, False)
    r_ref[...] = ft_ref[...].astype(BF16)
    zt_ref[0:1, :] = (gt_ref[2:3, :] - 2.0) * ROOT
    zt_ref[1:2, :] = gt_ref[1:2, :]
    l_ref[...] = jnp.transpose(fs_ref[...]).astype(BF16)
    term = lax.broadcasted_iota(jnp.int32, (TERMS, 128), 0)
    pick_z = ((term >= 18) & (term < 21)).astype(BF16)
    pick_y = ((term == 6) | (term == 10) | (term == 11)).astype(BF16)

    def spread(i, carry):
        at = pl.ds(pl.multiple_of(i * 512, 512), 512)
        left = l_ref[at, :]
        zb_ref[at, :] = jnp.dot(left, pick_z, preferred_element_type=F32) * ROOT
        yb_ref[at, :] = (jnp.dot(left, pick_y, preferred_element_type=F32) + 0.25) * (4.0 * SQUARE)
        return carry

    lax.fori_loop(0, SOURCES // 512, spread, 0, unroll=SOURCES // 512)

    def make_tile(at, block):
        start = pl.multiple_of(block * PIECE, PIECE)
        rest = jnp.dot(l_ref[at, :], r_ref[:, pl.ds(start, PIECE)], preferred_element_type=F32)
        zb, yb = zb_ref[at, :], yb_ref[at, :]
        near, far = [], []
        for c in range(PIECE // 128):
            lanes = pl.ds(start + c * 128, 128)
            dz = zb - zt_ref[0:1, lanes]
            squared = dz * dz + rest[:, c * 128 : (c + 1) * 128]
            near.append(lax.rsqrt(squared).astype(BF16))
            far.append(lax.rsqrt(squared + yb * zt_ref[1:2, lanes]).astype(BF16))
        near, far = jnp.concatenate(near, 1), jnp.concatenate(far, 1)
        a_ref[at, pl.ds(start, PIECE)] = near
        b_ref[at, pl.ds(start, PIECE)] = far
        return near, far

    def swap(value):
        return jnp.concatenate([value[RHS:], value[:RHS]], 0)

    def build(block):
        def step(i, carry):
            make_tile(pl.ds(pl.multiple_of(i * CHUNK, CHUNK), CHUNK), block)
            return carry

        lax.fori_loop(0, SOURCES // CHUNK, step, 0, unroll=SOURCES // CHUNK)

    def build_and_apply(block):
        def step(i, total):
            at = pl.ds(pl.multiple_of(i * CHUNK, CHUNK), CHUNK)
            near, far = make_tile(at, block)
            part = j_ref[0, :, at]
            total += jnp.dot(part, near, preferred_element_type=F32)
            return total + swap(jnp.dot(part, far, preferred_element_type=F32))

        zero = jnp.zeros((2 * RHS, PIECE), F32)
        return lax.fori_loop(0, SOURCES // CHUNK, step, zero, unroll=SOURCES // CHUNK)

    def apply(which, block):
        at = pl.ds(pl.multiple_of(block * PIECE, PIECE), PIECE)
        part = j_ref[which]
        return jnp.dot(part, a_ref[:, at], preferred_element_type=F32) + swap(
            jnp.dot(part, b_ref[:, at], preferred_element_type=F32)
        )

    def block_of(i):
        reach = (i + 1) // 2
        return (depth + 4 + reach * (2 * ((i + 1) % 2) - 1)) % BLOCKS

    def hand_over(i, carry):
        build(block_of(i))

        @pl.when(i == BLOCKS - 2)
        def _():
            for away in NEAREST:
                take(0, away)

        return carry

    pl.semaphore_wait(barrier, jnp.where(home == own_set, 15, 16) + SENDERS + 1 + 7)
    currents_start()
    lax.fori_loop(FUSED, BLOCKS, hand_over, 0)
    for away in NEAREST:
        take_other(0, away)

    def first(i, carry):
        block = block_of(i)
        part_store(0, block, build_and_apply(block))
        return carry

    lax.fori_loop(0, FUSED, first, 0)

    def rest(i, carry):
        block = block_of(i)
        part_store(0, block, apply(0, block))
        return carry

    lax.fori_loop(FUSED, BLOCKS, rest, 0)
    residual = right_ref[...] - part_sum(0)
    out_ref[0:RHS] = residual
    own_ref[...] = residual.astype(BF16)

    gather_start()

    def product(chunk, columns):
        part = j_ref[1, :, chunk]
        return jnp.dot(part, a_ref[chunk, columns], preferred_element_type=F32) + swap(
            jnp.dot(part, b_ref[chunk, columns], preferred_element_type=F32)
        )

    def sum_chunk(chunk, fresh):
        def step(i, carry):
            columns = pl.ds(pl.multiple_of(i * PART, PART), PART)
            total = product(chunk, columns)
            v_ref[:, columns] = total if fresh else v_ref[:, columns] + total
            return carry

        lax.fori_loop(0, TARGETS // PART, step, 0, unroll=TARGETS // PART)

    take(1, 2)
    sum_chunk(chunk_at(core, 2), True)
    take(1, 1)
    sum_chunk(chunk_at(core, 1), False)
    take(1, 3)
    take(1, 0)
    sum_chunk(chunk_at(core, 3), False)
    take_other(1, 2)
    sum_chunk(chunk_at(1 - core, 2), False)
    sum_chunk(chunk_at(core, 0), False)
    take_other(1, 1)
    sum_chunk(chunk_at(1 - core, 1), False)
    for away in (3, 0):
        take_other(1, away)

    def second(i, carry):
        block = block_of(i)
        columns = pl.ds(pl.multiple_of(block * PIECE, PIECE), PIECE)
        total = v_ref[:, columns]
        for away in (3, 0):
            total += product(chunk_at(1 - core, away), columns)
        part_store(1, block, total)
        return carry

    lax.fori_loop(0, BLOCKS, second, 0, unroll=4)

    def currents_left(i, carry):
        currents_copy(i).wait_send()
        return carry

    lax.fori_loop(1, 8, currents_left, 0)

    def gathered(i, carry):
        @pl.when(jnp.logical_not(is_self(*taker(i))))
        def _():
            gather_copy(i).wait_send()

        return carry

    lax.fori_loop(0, 16, gathered, 0)
    for which in range(2):

        for away in NEAREST:
            core_copy(which, away).wait_send()

        def parted(block, carry):
            for half in range(2):
                part_copy(which, half, block).wait_send()

            return carry

        lax.fori_loop(0, BLOCKS, parted, 0)

    out_ref[RHS : 2 * RHS] = part_sum(1)


def on_device(currents, right_side, geometry):
    vmem = pl.BlockSpec(memory_space=pltpu.VMEM)
    both = pl.pallas_call(
        kernel,
        out_shape=jax.ShapeDtypeStruct((2 * RHS, PIECE), F32),
        in_specs=[vmem, vmem, pl.BlockSpec(memory_space=pl.ANY)],
        out_specs=vmem,
        scratch_shapes=[
            pltpu.VMEM((SOURCES, TARGETS), BF16),
            pltpu.VMEM((SOURCES, TARGETS), BF16),
            pltpu.VMEM((4, SOURCES), F32),
            pltpu.VMEM((4, TARGETS), F32),
            pltpu.VMEM((TERMS, SOURCES), F32),
            pltpu.VMEM((TERMS, TARGETS), F32),
            pltpu.VMEM((SOURCES, TERMS), BF16),
            pltpu.VMEM((TERMS, TARGETS), BF16),
            pltpu.VMEM((SOURCES, 128), F32),
            pltpu.VMEM((SOURCES, 128), F32),
            pltpu.VMEM((2, TARGETS), F32),
            pltpu.VMEM((2, RHS, PART), BF16),
            pltpu.VMEM((RHS, PIECE), BF16),
            pltpu.VMEM((2, 2 * RHS, SOURCES), BF16),
            pltpu.VMEM((2 * RHS, TARGETS), F32),
            pltpu.VMEM((2, 2 * RHS, TARGETS), BF16),
            pltpu.VMEM((2, SENDERS, RHS, PIECE), BF16),
            pltpu.SemaphoreType.DMA((2,)),
            pltpu.SemaphoreType.DMA((2, 16)),
            pltpu.SemaphoreType.DMA((2, 4)),
            pltpu.SemaphoreType.DMA((2, 4)),
            pltpu.SemaphoreType.DMA((2, 4)),
            pltpu.SemaphoreType.DMA((2, 2, BLOCKS)),
            pltpu.SemaphoreType.DMA((2,)),
        ],
        compiler_params=pltpu.CompilerParams(
            collective_id=0, has_side_effects=True, vmem_limit_bytes=58 * 1024 * 1024
        ),
        name="peec_pair_products",
    )(currents, right_side, geometry)
    return both[:RHS], both[RHS:]


def solution(mesh):
    placed = (P(None, ("mirror", "rows")), P(None, ("mirror", "rows", "cols")), P())
    return jax.shard_map(
        on_device,
        mesh=mesh,
        in_specs=placed,
        out_specs=(P(None, ("mirror", "rows", "cols")), P(None, ("mirror", "rows", "cols"))),
        check_vma=False,
    )
```

```python
import functools

import jax
import jax.numpy as jnp
from jax import lax
from jax.experimental import pallas as pl
from jax.experimental.pallas import tpu as pltpu
from jax.sharding import PartitionSpec as P

MESH = pl.DeviceIdType.MESH
F32, BF16 = jnp.float32, jnp.bfloat16
HALF = 65536
RHS = 16
PIECE = 256
SOURCES = 4096
TARGETS = 2048
PIECES = SOURCES // PIECE
PART = 2 * PIECE
BLOCKS = TARGETS // PIECE
TERMS = 32
SQUARE = 2.0**17
ROOT = 2.0**8.5
CHUNK = 256
SENDERS = 16
NEAREST = (2, 1, 3, 0)
FUSED = 4


def split3(value):
    high = value.astype(BF16).astype(F32)
    rest = value - high
    middle = rest.astype(BF16).astype(F32)
    return high, middle, (rest - middle).astype(BF16).astype(F32)


def store_terms(geo, terms, source):
    across = geo[0:1, :] - 0.5
    height = geo[1:2, :] - 0.25
    size = geo[3:4, :]
    own = across * across + height * height + size * size
    xs, ys, qs = split3(across), split3(height), split3(own)
    one = jnp.ones_like(across)
    if source:
        zs = split3(geo[2:3, :] - 2.0)
        rows = [v[i] for v in (xs, ys) for i in (0, 0, 1, 0, 2, 1)]
        rows += [*qs, one, one, one, *zs]
    else:
        rows = [v[i] * (-2.0 * SQUARE) for v in (xs, ys) for i in (0, 1, 0, 2, 0, 1)]
        rows += [one * SQUARE] * 3 + [v * SQUARE for v in qs]
    for k in range(TERMS):
        terms[k : k + 1, :] = rows[k] if k < len(rows) else jnp.zeros_like(across)


def kernel(
    cur_ref, right_ref, geo_ref, out_ref,
    a_ref, b_ref, gs_ref, gt_ref, fs_ref, ft_ref, l_ref, r_ref, zb_ref, yb_ref, zt_ref,
    cur_pair_ref, own_ref, j_ref, v_ref, w_ref, p_ref,
    geo_sem, gather_send, gather_recv, core_send, core_recv, part_send, part_recv,
):
    mirror = lax.axis_index("mirror")
    row = lax.axis_index("rows")
    col = lax.axis_index("cols")
    core = row % 2
    depth = row // 8
    line = (row // 2) % 4
    across = (line + 2) % 4
    own_set = (mirror + line) % 2
    home = col // 2
    slot = core * 8 + line * 2 + col % 2
    me = mirror * 8 + depth

    barrier = pltpu.get_barrier_semaphore()

    def greet(other):
        pl.semaphore_signal(barrier, inc=1, device_id=other, device_id_type=MESH)

    def greet_source(k, carry):
        other = (k // 8, depth * 8 + (k // 2) % 4 * 2 + core, own_set * 2 + k % 2)

        @pl.when(jnp.logical_not(is_self(*other)))
        def _():
            greet(other)

        return carry

    def is_self(half, other, column):
        return jnp.logical_and(jnp.logical_and(half == mirror, other == row), column == col)

    def greet_part(k, carry):
        greet((k // 8, k % 8 * 8 + across * 2 + core, col))
        return carry

    def along_y(i):
        other = (mirror * 4 + line + i) % 8
        return (other // 4, depth * 8 + other % 4 * 2 + core, col), (other // 4 + other % 4) % 2

    def greet_column(i, carry):
        greet(along_y(i)[0])
        return carry

    sibling = (mirror, row + 1 - 2 * core, col)
    lax.fori_loop(1, 8, greet_column, 0)
    lax.fori_loop(0, 16, greet_source, 0)
    lax.fori_loop(0, SENDERS, greet_part, 0)
    greet(sibling)

    def source_geo(k, carry):
        start = (depth * 8 + k % 4 * 2 + k // 4) * 1024 + own_set * PART
        pltpu.make_async_copy(
            geo_ref.at[:, pl.ds(pl.multiple_of(start, PART), PART)],
            gs_ref.at[:, pl.ds(pl.multiple_of(k * PART, PART), PART)],
            geo_sem.at[0],
        ).start()
        return carry

    def target_geo(k, carry):
        start = (k * 8 + across * 2 + core) * 1024 + col * PIECE
        pltpu.make_async_copy(
            geo_ref.at[:, pl.ds(pl.multiple_of(start, PIECE), PIECE)],
            gt_ref.at[:, pl.ds(pl.multiple_of(k * PIECE, PIECE), PIECE)],
            geo_sem.at[1],
        ).start()
        return carry

    lax.fori_loop(0, SOURCES // PART, source_geo, 0)
    lax.fori_loop(0, BLOCKS, target_geo, 0)
    for half in range(2):
        cur_pair_ref[half] = cur_ref[:, half * PART : (half + 1) * PART]

    def currents_part():
        rows = pl.ds(pl.multiple_of(mirror * RHS, RHS), RHS)
        return j_ref.at[0, rows, pl.ds(pl.multiple_of((core * 4 + line) * PART, PART), PART)]

    def currents_copy(i):
        device, half = along_y(i)
        return pltpu.make_async_remote_copy(
            src_ref=cur_pair_ref.at[half],
            dst_ref=currents_part(),
            send_sem=gather_send.at[0, i],
            recv_sem=gather_recv.at[0, line],
            device_id=device,
            device_id_type=MESH,
        )

    def currents_start():
        def send(i, carry):
            currents_copy(i).start()
            return carry

        lax.fori_loop(1, 8, send, 0)
        pltpu.make_async_copy(cur_pair_ref.at[own_set], currents_part(), gather_recv.at[0, line]).start()

    def piece_at():
        rows = pl.ds(pl.multiple_of(mirror * RHS, RHS), RHS)
        return j_ref.at[1, rows, pl.ds(pl.multiple_of(slot * PIECE, PIECE), PIECE)]

    def gather_copy(i):
        return pltpu.make_async_remote_copy(
            src_ref=own_ref,
            dst_ref=piece_at(),
            send_sem=gather_send.at[1, i],
            recv_sem=gather_recv.at[1, line],
            device_id=taker(i),
            device_id_type=MESH,
        )

    def taker(i):
        other = (line + 2 + i // 4) % 4
        return (home + other) % 2, depth * 8 + other * 2 + core, (col + i) % 4

    def gather_start():
        def send(i, carry):
            @pl.when(jnp.logical_not(is_self(*taker(i))))
            def _():
                gather_copy(i).start()

            return carry

        lax.fori_loop(0, 16, send, 0)

        @pl.when(home == own_set)
        def _():
            pltpu.make_async_copy(own_ref, piece_at(), gather_recv.at[1, line]).start()

    def chunk_at(side, away):
        start = side * (SOURCES // 2) + (line + away) % 4 * PART
        return pl.ds(pl.multiple_of(start, PART), PART)

    def core_copy(which, away):
        part = j_ref.at[which, :, chunk_at(core, away)]
        return pltpu.make_async_remote_copy(
            src_ref=part,
            dst_ref=part,
            send_sem=core_send.at[which, (line + away) % 4],
            recv_sem=core_recv.at[which, (line + away) % 4],
            device_id=sibling,
            device_id_type=MESH,
        )

    def take(which, away):
        part = j_ref.at[which, :, chunk_at(core, away)]
        pltpu.make_async_copy(part, part, gather_recv.at[which, (line + away) % 4]).wait()
        core_copy(which, away).start()

    def take_other(which, away):
        part = j_ref.at[which, :, chunk_at(1 - core, away)]
        pltpu.make_async_copy(part, part, core_recv.at[which, (line + away) % 4]).wait()

    def part_copy(which, half, block):
        start = pl.multiple_of(block * PIECE, PIECE)
        return pltpu.make_async_remote_copy(
            src_ref=w_ref.at[which, pl.ds(half * RHS, RHS), pl.ds(start, PIECE)],
            dst_ref=p_ref.at[which, me],
            send_sem=part_send.at[which, half, block],
            recv_sem=part_recv.at[which],
            device_id=(half, block * 8 + across * 2 + core, col),
            device_id_type=MESH,
        )

    def part_store(which, block, total):
        start = pl.multiple_of(block * PIECE, PIECE)
        w_ref[which, :, pl.ds(start, PIECE)] = total.astype(BF16)
        for half in range(2):
            part_copy(which, half, block).start()

    def part_sum(which):
        pltpu.make_async_copy(p_ref.at[which], p_ref.at[which], part_recv.at[which]).wait()
        total = p_ref[which, 0].astype(F32)
        for k in range(1, SENDERS):
            total += p_ref[which, k].astype(F32)
        return total

    pltpu.make_async_copy(gs_ref, gs_ref, geo_sem.at[0]).wait()
    pltpu.make_async_copy(gt_ref, gt_ref, geo_sem.at[1]).wait()
    store_terms(gs_ref, fs_ref, True)
    store_terms(gt_ref, ft_ref, False)
    r_ref[...] = ft_ref[...].astype(BF16)
    zt_ref[0:1, :] = (gt_ref[2:3, :] - 2.0) * ROOT
    zt_ref[1:2, :] = gt_ref[1:2, :]
    l_ref[...] = jnp.transpose(fs_ref[...]).astype(BF16)
    term = lax.broadcasted_iota(jnp.int32, (TERMS, 128), 0)
    pick_z = ((term >= 18) & (term < 21)).astype(BF16)
    pick_y = ((term == 6) | (term == 10) | (term == 11)).astype(BF16)

    def spread(i, carry):
        at = pl.ds(pl.multiple_of(i * 512, 512), 512)
        left = l_ref[at, :]
        zb_ref[at, :] = jnp.dot(left, pick_z, preferred_element_type=F32) * ROOT
        yb_ref[at, :] = (jnp.dot(left, pick_y, preferred_element_type=F32) + 0.25) * (4.0 * SQUARE)
        return carry

    lax.fori_loop(0, SOURCES // 512, spread, 0, unroll=SOURCES // 512)

    def make_tile(at, block):
        start = pl.multiple_of(block * PIECE, PIECE)
        rest = jnp.dot(l_ref[at, :], r_ref[:, pl.ds(start, PIECE)], preferred_element_type=F32)
        zb, yb = zb_ref[at, :], yb_ref[at, :]
        near, far = [], []
        for c in range(PIECE // 128):
            lanes = pl.ds(start + c * 128, 128)
            dz = zb - zt_ref[0:1, lanes]
            squared = dz * dz + rest[:, c * 128 : (c + 1) * 128]
            near.append(lax.rsqrt(squared).astype(BF16))
            far.append(lax.rsqrt(squared + yb * zt_ref[1:2, lanes]).astype(BF16))
        near, far = jnp.concatenate(near, 1), jnp.concatenate(far, 1)
        a_ref[at, pl.ds(start, PIECE)] = near
        b_ref[at, pl.ds(start, PIECE)] = far
        return near, far

    def swap(value):
        return jnp.concatenate([value[RHS:], value[:RHS]], 0)

    def build(block):
        def step(i, carry):
            make_tile(pl.ds(pl.multiple_of(i * CHUNK, CHUNK), CHUNK), block)
            return carry

        lax.fori_loop(0, SOURCES // CHUNK, step, 0, unroll=SOURCES // CHUNK)

    def build_and_apply(block):
        def step(i, total):
            at = pl.ds(pl.multiple_of(i * CHUNK, CHUNK), CHUNK)
            near, far = make_tile(at, block)
            part = j_ref[0, :, at]
            total += jnp.dot(part, near, preferred_element_type=F32)
            return total + swap(jnp.dot(part, far, preferred_element_type=F32))

        zero = jnp.zeros((2 * RHS, PIECE), F32)
        return lax.fori_loop(0, SOURCES // CHUNK, step, zero, unroll=SOURCES // CHUNK)

    def apply(which, block):
        at = pl.ds(pl.multiple_of(block * PIECE, PIECE), PIECE)
        part = j_ref[which]
        return jnp.dot(part, a_ref[:, at], preferred_element_type=F32) + swap(
            jnp.dot(part, b_ref[:, at], preferred_element_type=F32)
        )

    def block_of(i):
        reach = (i + 1) // 2
        return (depth + 4 + reach * (2 * ((i + 1) % 2) - 1)) % BLOCKS

    def hand_over(i, carry):
        build(block_of(i))

        @pl.when(i == BLOCKS - 2)
        def _():
            for away in NEAREST:
                take(0, away)

        return carry

    pl.semaphore_wait(barrier, jnp.where(home == own_set, 15, 16) + SENDERS + 1 + 7)
    currents_start()
    lax.fori_loop(FUSED, BLOCKS, hand_over, 0)
    for away in NEAREST:
        take_other(0, away)

    def first(i, carry):
        block = block_of(i)
        part_store(0, block, build_and_apply(block))
        return carry

    lax.fori_loop(0, FUSED, first, 0)

    def rest(i, carry):
        block = block_of(i)
        part_store(0, block, apply(0, block))
        return carry

    lax.fori_loop(FUSED, BLOCKS, rest, 0)
    residual = right_ref[...] - part_sum(0)
    out_ref[0:RHS] = residual
    own_ref[...] = residual.astype(BF16)

    gather_start()

    def product(chunk, columns):
        part = j_ref[1, :, chunk]
        return jnp.dot(part, a_ref[chunk, columns], preferred_element_type=F32) + swap(
            jnp.dot(part, b_ref[chunk, columns], preferred_element_type=F32)
        )

    def sum_chunk(chunk, fresh):
        def step(i, carry):
            columns = pl.ds(pl.multiple_of(i * PART, PART), PART)
            total = product(chunk, columns)
            v_ref[:, columns] = total if fresh else v_ref[:, columns] + total
            return carry

        lax.fori_loop(0, TARGETS // PART, step, 0, unroll=TARGETS // PART)

    take(1, 2)
    sum_chunk(chunk_at(core, 2), True)
    take(1, 1)
    sum_chunk(chunk_at(core, 1), False)
    take(1, 3)
    take(1, 0)
    sum_chunk(chunk_at(core, 3), False)
    take_other(1, 2)
    sum_chunk(chunk_at(1 - core, 2), False)
    sum_chunk(chunk_at(core, 0), False)
    take_other(1, 1)
    sum_chunk(chunk_at(1 - core, 1), False)
    for away in (3, 0):
        take_other(1, away)

    def second(i, carry):
        block = block_of(i)
        columns = pl.ds(pl.multiple_of(block * PIECE, PIECE), PIECE)
        total = v_ref[:, columns]
        for away in (3, 0):
            total += product(chunk_at(1 - core, away), columns)
        part_store(1, block, total)
        return carry

    lax.fori_loop(0, BLOCKS, second, 0, unroll=4)

    def currents_left(i, carry):
        currents_copy(i).wait_send()
        return carry

    lax.fori_loop(1, 8, currents_left, 0)

    def gathered(i, carry):
        @pl.when(jnp.logical_not(is_self(*taker(i))))
        def _():
            gather_copy(i).wait_send()

        return carry

    lax.fori_loop(0, 16, gathered, 0)
    for which in range(2):

        for away in NEAREST:
            core_copy(which, away).wait_send()

        def parted(block, carry):
            for half in range(2):
                part_copy(which, half, block).wait_send()

            return carry

        lax.fori_loop(0, BLOCKS, parted, 0)

    out_ref[RHS : 2 * RHS] = part_sum(1)


def on_device(currents, right_side, geometry):
    vmem = pl.BlockSpec(memory_space=pltpu.VMEM)
    both = pl.pallas_call(
        kernel,
        out_shape=jax.ShapeDtypeStruct((2 * RHS, PIECE), F32),
        in_specs=[vmem, vmem, pl.BlockSpec(memory_space=pl.ANY)],
        out_specs=vmem,
        scratch_shapes=[
            pltpu.VMEM((SOURCES, TARGETS), BF16),
            pltpu.VMEM((SOURCES, TARGETS), BF16),
            pltpu.VMEM((4, SOURCES), F32),
            pltpu.VMEM((4, TARGETS), F32),
            pltpu.VMEM((TERMS, SOURCES), F32),
            pltpu.VMEM((TERMS, TARGETS), F32),
            pltpu.VMEM((SOURCES, TERMS), BF16),
            pltpu.VMEM((TERMS, TARGETS), BF16),
            pltpu.VMEM((SOURCES, 128), F32),
            pltpu.VMEM((SOURCES, 128), F32),
            pltpu.VMEM((2, TARGETS), F32),
            pltpu.VMEM((2, RHS, PART), BF16),
            pltpu.VMEM((RHS, PIECE), BF16),
            pltpu.VMEM((2, 2 * RHS, SOURCES), BF16),
            pltpu.VMEM((2 * RHS, TARGETS), F32),
            pltpu.VMEM((2, 2 * RHS, TARGETS), BF16),
            pltpu.VMEM((2, SENDERS, RHS, PIECE), BF16),
            pltpu.SemaphoreType.DMA((2,)),
            pltpu.SemaphoreType.DMA((2, 16)),
            pltpu.SemaphoreType.DMA((2, 4)),
            pltpu.SemaphoreType.DMA((2, 4)),
            pltpu.SemaphoreType.DMA((2, 4)),
            pltpu.SemaphoreType.DMA((2, 2, BLOCKS)),
            pltpu.SemaphoreType.DMA((2,)),
        ],
        compiler_params=pltpu.CompilerParams(
            collective_id=0, has_side_effects=True, vmem_limit_bytes=58 * 1024 * 1024
        ),
        name="peec_pair_products",
    )(currents, right_side, geometry)
    return both[:RHS], both[RHS:]


def solution(mesh):
    placed = (P(None, ("mirror", "rows")), P(None, ("mirror", "rows", "cols")), P())
    return jax.shard_map(
        on_device,
        mesh=mesh,
        in_specs=placed,
        out_specs=(P(None, ("mirror", "rows", "cols")), P(None, ("mirror", "rows", "cols"))),
        check_vma=False,
    )
```
